256 devices in a mesh: lat: 16 (over y_lo, x, core), lon: 16 (over z, y_hi).
Axes of the slice: x: 4, y: 4 (y_hi: 2, y_lo: 2; y = y_hi * 2 + y_lo), z: 8, core: 2. Of those that a mesh axis runs over, the one named last changes fastest.
Arguments:
- fields: bfloat16 [512, 512, 256], P('lat', 'lon'), may hold values from -6 to 6
- w_conv1: bfloat16 [3, 3, 256, 256], replicated, may hold values from -0.125 to 0.125
- b_conv1: float32 [256], replicated, may hold values from -3 to 3
- w_conv2: bfloat16 [3, 3, 256, 256], replicated, may hold values from -0.125 to 0.125
- b_conv2: float32 [256], replicated, may hold values from -3 to 3
- w_query: bfloat16 [256, 256], replicated, may hold values from -16 to 16
- w_key: bfloat16 [256, 64], replicated, may hold values from -1 to 1
- w_value: bfloat16 [256, 64], replicated, may hold values from -0.375 to 0.375
- w_out: bfloat16 [256, 256], replicated, may hold values from -0.375 to 0.375
- rotation: int32 [16, 16], replicated, may hold values from 0 to 3
- owner: int32 [16, 16], replicated, may hold values from 0 to 15, as said below
- counts: int32 [512], replicated, may hold values from 4 to 512
Outputs:
- fields_out: bfloat16 [512, 512, 256], P('lat', 'lon')
The draws below stay inside these ranges and needn't reach their ends.
Inputs may be any that keep to these rules, and one draw needn't show every extreme that they name: Each row of owner holds every number from 0 to 15 exactly once.
All inputs are finite; a program needn't handle non-finite values.
Results may differ from the reference program's by a relative error of at most 0.014.
Values may be sent and summed in bfloat16 or wider, within the bound.
A program may use at most 64 MiB of HBM per device.

```python
import math
import jax
import jax.numpy as jnp
from jax import lax

C = 256
HEADS = 4
HEAD_DIM = 64
P_SIZE = 32
CYCLES = 512
LONC = 512
N_LAT = 16
N_LON = 16


def weight_pair(key):
    key_draw = jax.random.normal(jax.random.fold_in(key, 101), (C, HEAD_DIM), jnp.float32) * C ** (-0.5)
    key_draw = jnp.clip(key_draw, -1.0, 1.0)
    base = jax.random.normal(jax.random.fold_in(key, 102), (C, C), jnp.float32) * C ** (-0.5)
    query_draw = 3.0 * base
    query_draw = jnp.clip(query_draw, -16.0, 16.0)
    return (query_draw, key_draw)


def draw_w_query(key, part):
    return weight_pair(key)[0].astype(jnp.bfloat16)


def draw_w_key(key, part):
    return weight_pair(key)[1].astype(jnp.bfloat16)


def draw_owner(key, part):
    band_keys = jax.random.split(key, N_LAT)
    return jax.vmap(lambda k: jax.random.permutation(k, N_LON))(band_keys).astype(jnp.int32)


def draw_counts(key, part):
    row_ids = jnp.arange(CYCLES, dtype=jnp.int32)
    from_pole = jnp.minimum(row_ids, CYCLES - 1 - row_ids)
    extra = jax.random.randint(key, (CYCLES,), 0, 2 * P_SIZE, dtype=jnp.int32) * (from_pole > 0).astype(jnp.int32)
    return jnp.minimum(LONC, 4 * (from_pole + 1) + extra).astype(jnp.int32)


def place_ends(entries, rng, low, top_value):
    index_at = [jax.random.randint(jax.random.fold_in(rng, axis), (), 0, length) for axis, length in enumerate(entries.shape)]
    main_axis = entries.shape.index(max(entries.shape))
    next_to = index_at[:main_axis] + [(index_at[main_axis] + 1) % entries.shape[main_axis]] + index_at[main_axis + 1:]
    return entries.at[tuple(index_at)].set(low).at[tuple(next_to)].set(top_value)


def level_of(rng, shape, cuts, least, largest):
    gain = 1.0
    for dim, parts in cuts:
        steps = jax.random.uniform(jax.random.fold_in(jax.random.fold_in(rng, 6), dim), (parts,), jnp.float32, least / len(cuts), largest / len(cuts))
        gain = gain * jnp.repeat(jnp.exp(steps), shape[dim] // parts).reshape((-1,) + (1,) * (len(shape) - 1 - dim))
    return gain


def centred(rng, dims, spread, limit, pieces=(), kind=jnp.bfloat16):
    entries = jax.random.normal(rng, dims, jnp.float32) * spread
    if len(pieces) > 0:
        entries = level_of(rng, dims, pieces, -0.22, 0.18) * entries
    return jnp.clip(entries, min=-limit, max=limit).astype(kind)


def setup_inputs(seed: int = 0) -> dict:
    key_of = jax.random.split(jax.random.key(seed), 13)
    return {
        "fields": centred(key_of[0], (CYCLES, LONC, C), 1.0, 6.0, ((0, 16), (1, 16))),
        "w_conv1": centred(key_of[1], (3, 3, C, C), (9 * C) ** -0.5, 0.125),
        "b_conv1": centred(key_of[2], (C,), 0.5, 3.0, (), jnp.float32),
        "w_conv2": centred(key_of[3], (3, 3, C, C), (9 * C) ** -0.5, 0.125),
        "b_conv2": centred(key_of[4], (C,), 0.5, 3.0, (), jnp.float32),
        "w_query": draw_w_query(jax.random.fold_in(key_of[12], 71), 0),
        "w_key": draw_w_key(jax.random.fold_in(key_of[12], 71), 0),
        "w_value": centred(key_of[7], (C, HEAD_DIM), C ** -0.5, 0.375),
        "w_out": centred(key_of[8], (C, C), C ** -0.5, 0.375),
        "rotation": place_ends(jax.random.randint(key_of[9], (N_LAT, N_LON), 0, 4), jax.random.fold_in(key_of[9], 1), 0, 3).astype(jnp.int32),
        "owner": draw_owner(jax.random.fold_in(key_of[12], 71), 0),
        "counts": draw_counts(jax.random.fold_in(key_of[12], 71), 0),
    }


def inverse_owner(owner):
    shards = jnp.arange(N_LON, dtype=jnp.int32)
    matches = owner[:, None, :] == shards[None, :, None]
    return lax.optimization_barrier(jnp.sum(jnp.where(matches, shards[None, None, :], 0), axis=2)).astype(jnp.int32)

def turn_blocks(blocks, quarter_turns):
    result = blocks
    for k in (1, 2, 3):
        turned = jnp.rot90(blocks, k, axes=(2, 3))
        result = jnp.where((quarter_turns % 4 == k)[:, :, None, None, None], turned, result)
    return result

def to_true(fields, rotation, owner):
    blocks = fields.reshape(N_LAT, P_SIZE, N_LON, P_SIZE, C).transpose(0, 2, 1, 3, 4)
    upright = turn_blocks(blocks, (4 - rotation) % 4)
    placed = jnp.take_along_axis(upright, inverse_owner(owner)[:, :, None, None, None], axis=1)
    return placed.transpose(0, 2, 1, 3, 4).reshape(CYCLES, LONC, C)

def from_true(grid, rotation, owner):
    blocks = grid.reshape(N_LAT, P_SIZE, N_LON, P_SIZE, C).transpose(0, 2, 1, 3, 4)
    holder_blocks = jnp.take_along_axis(blocks, owner[:, :, None, None, None], axis=1)
    return turn_blocks(holder_blocks, rotation).transpose(0, 2, 1, 3, 4).reshape(CYCLES, LONC, C)

def convolve(field, weight, bias):
    wrapped = jnp.concatenate([field[:, -1:], field, field[:, :1]], axis=1)
    padded = jnp.pad(wrapped, ((1, 1), (0, 0), (0, 0)))
    total = jnp.zeros((CYCLES * LONC, C), jnp.float32) + bias.astype(jnp.float32)
    for i in range(3):
        for j in range(3):
            window = padded[i:i + CYCLES, j:j + LONC].reshape(CYCLES * LONC, C)
            total = total + jnp.dot(window, weight[i, j], preferred_element_type=jnp.float32)
    return total.reshape(CYCLES, LONC, C)

def attend_row(operands):
    query_row, kv_row, live_row = operands
    heads_q = query_row.reshape(LONC, HEADS, HEAD_DIM).astype(jnp.float32)
    keys_row = kv_row[:, :HEAD_DIM].astype(jnp.float32)
    values_row = kv_row[:, HEAD_DIM:].astype(jnp.float32)
    scores = jnp.einsum('chd,kd->chk', heads_q, keys_row, precision=lax.Precision.HIGHEST) / math.sqrt(HEAD_DIM)
    scores = jnp.where(live_row[None, None, :] > 0, scores, -jnp.inf)
    peak = lax.optimization_barrier(jnp.max(scores, axis=2, keepdims=True))
    expo = jnp.exp(scores - peak)
    total = lax.optimization_barrier(jnp.sum(expo, axis=2))
    weights = expo.astype(jnp.bfloat16)
    summed = jnp.einsum('chk,kd->chd', weights.astype(jnp.float32), values_row, precision=lax.Precision.HIGHEST)
    return (summed / total[:, :, None]).astype(jnp.bfloat16).reshape(LONC, C)

def reference(fields, w_conv1, b_conv1, w_conv2, b_conv2, w_query, w_key, w_value, w_out, rotation, owner, counts):
    grid = to_true(fields, rotation, owner)
    columns = jnp.arange(LONC, dtype=jnp.int32)
    live = (columns[None, :] < counts[:, None]).astype(jnp.float32)
    live_three = live[:, :, None]
    first = convolve(grid, w_conv1, b_conv1)
    act = (jax.nn.silu(first) * live_three).astype(jnp.bfloat16)
    second = convolve(act, w_conv2, b_conv2)
    mixed = ((grid.astype(jnp.float32) + second) * live_three).astype(jnp.bfloat16)
    flat = mixed.reshape(CYCLES * LONC, C).astype(jnp.float32)
    normed = (flat * lax.rsqrt(lax.optimization_barrier(jnp.mean(flat * flat, axis=1, keepdims=True)) + 1e-06)).astype(jnp.bfloat16)
    query = jnp.dot(normed, w_query, preferred_element_type=jnp.float32).astype(jnp.bfloat16)
    key_part = jnp.dot(normed, w_key, preferred_element_type=jnp.float32)
    value_part = jnp.dot(normed, w_value, preferred_element_type=jnp.float32)
    key_val = jnp.concatenate([key_part, value_part], axis=1).astype(jnp.bfloat16)
    attended = lax.map(attend_row, (query.reshape(CYCLES, LONC, C), key_val.reshape(CYCLES, LONC, 2 * HEAD_DIM), live))
    update = jnp.dot(attended.reshape(CYCLES * LONC, C), w_out, preferred_element_type=jnp.float32).reshape(CYCLES, LONC, C)
    result = (mixed.astype(jnp.float32) + update * live_three).astype(jnp.bfloat16)
    return from_true(result, rotation, owner)
```

```python
import functools
import math

import jax
import jax.numpy as jnp
from jax import lax
from jax.experimental import pallas as pl
from jax.experimental.pallas import tpu as pltpu
from jax.sharding import PartitionSpec as P

MESH = pl.DeviceIdType.MESH
C = 256
HEADS = 4
HEAD_DIM = 64
SIDE = 32
COLS = 512
SEGS = 16
GROUPS = 256
PIECE = 2 * SIDE
BF16 = jnp.bfloat16
F32 = jnp.float32


def row_group(lat, lon):
    pair, core = lat // 2, lat % 2
    z, high = lon // 2, lon % 2
    place = z + high * (15 - 2 * z)
    place = place + (pair % 2) * (15 - 2 * place)
    return 32 * pair + 2 * place + core


def holder(group):
    pair, rest = group // 32, group % 32
    place, core = rest // 2, rest % 2
    place = place + (pair % 2) * (15 - 2 * place)
    high = place // 8
    z = place + high * (15 - 2 * place)
    return 2 * pair + core, 2 * z + high


def turned(block, base, step_i, step_j, first, count):
    cells = lax.broadcasted_iota(jnp.int32, (count, 1), 0) + first
    source = base + step_i * (cells // SIDE) + step_j * (cells % SIDE)
    spots = lax.broadcasted_iota(jnp.int32, (count, SIDE * SIDE), 1)
    pick = jnp.where(spots == source, 1.0, 0.0).astype(BF16)
    return jnp.dot(pick, block, preferred_element_type=F32).astype(BF16)


def steps_of(quarter, upright):
    n = SIDE
    odd_a = (n * (n - 1), 1, -n)
    odd_b = (n - 1, -1, n)
    one, three = (odd_a, odd_b) if upright else (odd_b, odd_a)
    table = [(0, n, 1), one, (n * n - 1, -n, -1), three]

    def chosen(at):
        value = table[0][at]
        for k in (1, 2, 3):
            value = jnp.where(quarter == k, table[k][at], value)
        return value

    return chosen(0), chosen(1), chosen(2)


def section(
    rotation_ref, inverse_ref, owner_ref, counts_ref,
    fields_ref, w1_hbm, b1_ref, w2_hbm, b2_ref,
    wq_ref, wk_ref, wv_ref, wo_ref,
    out_ref,
    upright, raw_up, raw, raw_down, rows, acts, result, outgoing, w1, w2, wkv,
    send_in, recv_in, send_halo, recv_halo, send_out, recv_out, local_sem, weight_sem,
):
    lat, lon = lax.axis_index("lat"), lax.axis_index("lon")
    group = row_group(lat, lon)
    band = group // 16
    mine = band == lat
    barrier = pltpu.get_barrier_semaphore()

    def greet(device):
        @pl.when(jnp.logical_or(device[0] != lat, device[1] != lon))
        def _():
            pl.semaphore_signal(barrier, inc=1, device_id=device, device_id_type=MESH)

    def greet_all(j, carry):
        greet(holder(16 * lat + j))
        greet((band, j))
        return carry

    lax.fori_loop(0, 16, greet_all, 0)

    @pl.when(group > 0)
    def _():
        pl.semaphore_signal(barrier, inc=1, device_id=holder(group - 1), device_id_type=MESH)

    @pl.when(group < GROUPS - 1)
    def _():
        pl.semaphore_signal(barrier, inc=1, device_id=holder(group + 1), device_id_type=MESH)

    def weight_copies():
        for which, (source, target) in enumerate(((w1_hbm, w1), (w2_hbm, w2))):
            for i in range(3):
                for j in range(3):
                    yield pltpu.make_async_copy(
                        source.at[i, j],
                        target.at[pl.ds(C * i, C), pl.ds(C * j, C)],
                        weight_sem.at[which, 3 * i + j],
                    )

    for copy in weight_copies():
        copy.start()

    quarter = rotation_ref[lat, lon]
    base, step_i, step_j = steps_of(quarter, True)

    def turn(at, carry):
        part = turned(fields_ref[...], base, step_i, step_j, at * 256, 256)
        upright[pl.ds(4 * at, 4)] = part.reshape(4, PIECE, C)
        return carry

    lax.fori_loop(0, 4, turn, 0)

    @pl.when(group == 0)
    def _():
        raw_up[...] = jnp.zeros((SEGS, PIECE, C), BF16)

    @pl.when(group == GROUPS - 1)
    def _():
        raw_down[...] = jnp.zeros((SEGS, PIECE, C), BF16)

    key_part = wk_ref[...]
    value_part = wv_ref[...]
    blank = jnp.zeros((C, HEAD_DIM), BF16)
    wkv[...] = jnp.concatenate(
        [key_part, blank, blank, key_part, value_part, blank, blank, value_part], axis=1
    )

    own = jnp.where(mine, 1, 0)
    pl.semaphore_wait(
        barrier,
        2 * (16 - own) + jnp.where(group > 0, 1, 0) + jnp.where(group < GROUPS - 1, 1, 0),
    )

    def piece_copy(j):
        return pltpu.make_async_remote_copy(
            src_ref=upright.at[j],
            dst_ref=raw.at[lon],
            send_sem=send_in.at[j],
            recv_sem=recv_in.at[lon],
            device_id=holder(16 * lat + j),
            device_id_type=MESH,
        )

    def own_copy():
        return pltpu.make_async_copy(upright.at[group % 16], raw.at[lon], local_sem.at[0])

    @pl.when(mine)
    def _():
        own_copy().start()

    def send_piece(t, carry):
        j = (group + 1 + t) % 16

        @pl.when(16 * lat + j != group)
        def _():
            piece_copy(j).start()

        return carry

    lax.fori_loop(0, 16, send_piece, 0)

    def halo_copy(s, up):
        slot = 2 if up else 0
        return pltpu.make_async_remote_copy(
            src_ref=raw.at[s],
            dst_ref=(raw_down if up else raw_up).at[s],
            send_sem=send_halo.at[slot, s],
            recv_sem=recv_halo.at[slot, s],
            device_id=holder(group - 1 if up else group + 1),
            device_id_type=MESH,
        )

    def arrived(s):
        return pltpu.make_async_remote_copy(
            src_ref=upright.at[0],
            dst_ref=raw.at[s],
            send_sem=send_in.at[0],
            recv_sem=recv_in.at[s],
            device_id=(band, s),
            device_id_type=MESH,
        )

    def forward(t, carry):
        s = (lon + t) % 16
        here = jnp.logical_and(mine, s == lon)

        @pl.when(here)
        def _():
            own_copy().wait()

        @pl.when(jnp.logical_not(here))
        def _():
            arrived(s).wait_recv()

        @pl.when(group > 0)
        def _():
            halo_copy(s, True).start()

        @pl.when(group < GROUPS - 1)
        def _():
            halo_copy(s, False).start()

        return carry

    lax.fori_loop(0, 16, forward, 0)

    def place(slot):
        from_band = jnp.clip(group - 1 + slot, 0, GROUPS - 1) // 16
        for t in range(SEGS):
            s = inverse_ref[from_band, t]
            piece = (raw_up, raw, raw_down)[slot][s]
            for r in range(2):
                rows[pl.ds(SIDE * t, SIDE), pl.ds(C * (2 * slot + r), C)] = piece[
                    SIDE * r : SIDE * (r + 1)
                ]

    place(1)
    for copy in weight_copies():
        copy.wait()

    def wait_halo(s, carry):
        @pl.when(group < GROUPS - 1)
        def _():
            halo_copy(s, True).wait_recv()

        @pl.when(group > 0)
        def _():
            halo_copy(s, False).wait_recv()

        return carry

    lax.fori_loop(0, 16, wait_halo, 0)
    place(0)
    place(2)

    columns = lax.broadcasted_iota(jnp.int32, (COLS, 1), 0)

    def live_of(offset):
        row = 2 * group + offset
        inside = jnp.logical_and(row >= 0, row < 2 * GROUPS)
        count = jnp.where(inside, counts_ref[jnp.clip(row, 0, 2 * GROUPS - 1)], 0)
        return jnp.where(columns < count, 1.0, 0.0)

    def convolved(source, r, weight, bias_ref):
        taps = jnp.dot(
            source[:, C * r : C * (r + 3)], weight[...], preferred_element_type=F32
        )
        return (
            pltpu.roll(taps[:, :C], 1, 0)
            + taps[:, C : 2 * C]
            + pltpu.roll(taps[:, 2 * C :], COLS - 1, 0)
            + bias_ref[...]
        )

    def make_act(r):
        first = convolved(rows, r, w1, b1_ref)
        value = first / (1.0 + jnp.exp(-first))
        acts[:, C * r : C * (r + 1)] = (value * live_of(r - 1)).astype(BF16)

    scale = math.log2(math.e) / math.sqrt(HEAD_DIM)
    lanes = lax.broadcasted_iota(jnp.int32, (1, 2 * HEAD_DIM), 1)
    low = lanes < HEAD_DIM

    def make_row(r):
        live = live_of(r)
        second = convolved(acts, r, w2, b2_ref)
        grid = rows[:, C * (r + 2) : C * (r + 3)].astype(F32)
        mixed = ((grid + second) * live).astype(BF16)
        flat = mixed.astype(F32)
        mean = jnp.mean(flat * flat, axis=1, keepdims=True)
        normed = (flat * lax.rsqrt(mean + 1e-06)).astype(BF16)
        query = jnp.dot(normed, wq_ref[...], preferred_element_type=F32)
        key_val = jnp.dot(normed, wkv[...], preferred_element_type=F32)
        bias = jnp.where(live > 0, 0.0, -1e30)
        ones = jnp.broadcast_to(live, (COLS, 2 * HEAD_DIM)).astype(BF16)
        keys, values, marks = [], [], []
        for odd in range(2):
            spot = jnp.where(lanes == (0 if odd else HEAD_DIM), 1.0, 0.0)
            pair = key_val[:, 128 * odd : 128 * (odd + 1)]
            keys.append((pair + bias * spot).astype(BF16))
            pair = key_val[:, 256 + 128 * odd : 256 + 128 * (odd + 1)].astype(BF16)
            values.append(jnp.concatenate([pair, ones], axis=1))
            marks.append(spot)
        parts = []
        for h in range(HEADS):
            odd = h % 2
            pair = query[:, 128 * (h // 2) : 128 * (h // 2 + 1)]
            keep = jnp.logical_not(low) if odd else low
            head = jnp.where(keep, pair, marks[odd]).astype(BF16)
            scores = lax.dot_general(
                head, keys[odd], (((1,), (1,)), ((), ())), preferred_element_type=F32
            )
            peak = jnp.max(scores, axis=1, keepdims=True)
            weights = jnp.exp2((scores - peak) * scale).astype(BF16)
            summed = jnp.dot(weights, values[odd], preferred_element_type=F32)
            part = summed[:, :128] / summed[:, 128:]
            if odd:
                parts[-1] = parts[-1] + part
            else:
                parts.append(part)
        attended = jnp.concatenate(parts, axis=1).astype(BF16)
        update = jnp.dot(attended, wo_ref[...], preferred_element_type=F32)
        done = (mixed.astype(F32) + update * live).astype(BF16)
        result[r] = done.reshape(SEGS, SIDE, C)

    def return_copy(r, s):
        return pltpu.make_async_remote_copy(
            src_ref=outgoing.at[r, s],
            dst_ref=out_ref.at[group % 16, pl.ds(SIDE * r, SIDE)],
            send_sem=send_out.at[r, s],
            recv_sem=recv_out.at[r, group % 16],
            device_id=(band, s),
            device_id_type=MESH,
        )

    def return_own(r):
        return pltpu.make_async_copy(
            outgoing.at[r, lon],
            out_ref.at[group % 16, pl.ds(SIDE * r, SIDE)],
            local_sem.at[1 + r],
        )

    def send_row(r):
        for s in range(SEGS):
            outgoing[r, s] = result[r, owner_ref[band, s]]

        @pl.when(mine)
        def _():
            return_own(r).start()

        def send(t, carry):
            s = (lon + 1 + t) % 16

            @pl.when(jnp.logical_or(band != lat, s != lon))
            def _():
                return_copy(r, s).start()

            return carry

        lax.fori_loop(0, 16, send, 0)

    for r in range(3):
        make_act(r)
    make_row(0)
    send_row(0)
    make_act(3)
    make_row(1)
    send_row(1)

    def drain(t, carry):
        @pl.when(16 * lat + t != group)
        def _():
            piece_copy(t).wait_send()

        @pl.when(group > 0)
        def _():
            halo_copy(t, True).wait_send()

        @pl.when(group < GROUPS - 1)
        def _():
            halo_copy(t, False).wait_send()

        @pl.when(jnp.logical_or(band != lat, t != lon))
        def _():
            for r in range(2):
                return_copy(r, t).wait_send()

        @pl.when(16 * lat + t != group)
        def _():
            for r in range(2):
                pltpu.make_async_remote_copy(
                    src_ref=outgoing.at[r, 0],
                    dst_ref=out_ref.at[t, pl.ds(SIDE * r, SIDE)],
                    send_sem=send_out.at[r, 0],
                    recv_sem=recv_out.at[r, t],
                    device_id=holder(16 * lat + t),
                    device_id_type=MESH,
                ).wait_recv()

        return carry

    lax.fori_loop(0, 16, drain, 0)

    @pl.when(mine)
    def _():
        for r in range(2):
            return_own(r).wait()


def turn_back(rotation_ref, block_ref, out_ref):
    quarter = rotation_ref[lax.axis_index("lat"), lax.axis_index("lon")]
    base, step_i, step_j = steps_of(quarter, False)

    def turn(at, carry):
        out_ref[pl.ds(at * 256, 256)] = turned(
            block_ref[...], base, step_i, step_j, at * 256, 256
        )
        return carry

    lax.fori_loop(0, 4, turn, 0)


def inverse_owner(owner):
    shards = jnp.arange(owner.shape[1], dtype=jnp.int32)
    matches = owner[:, None, :] == shards[None, :, None]
    return jnp.sum(jnp.where(matches, shards[None, None, :], 0), axis=2)


def on_device(
    fields, w_conv1, b_conv1, w_conv2, b_conv2, w_query, w_key, w_value, w_out,
    rotation, owner, counts,
):
    smem = pl.BlockSpec(memory_space=pltpu.SMEM)
    vmem = pl.BlockSpec(memory_space=pltpu.VMEM)
    hbm = pl.BlockSpec(memory_space=pl.ANY)
    dma = pltpu.SemaphoreType.DMA
    block = pl.pallas_call(
        section,
        name="section",
        out_shape=jax.ShapeDtypeStruct((SEGS, PIECE, C), BF16),
        in_specs=[smem] * 4 + [vmem, hbm, vmem, hbm, vmem] + [vmem] * 4,
        out_specs=vmem,
        scratch_shapes=[
            pltpu.VMEM((SEGS, PIECE, C), BF16),
            pltpu.VMEM((SEGS, PIECE, C), BF16),
            pltpu.VMEM((SEGS, PIECE, C), BF16),
            pltpu.VMEM((SEGS, PIECE, C), BF16),
            pltpu.VMEM((COLS, 6 * C), BF16),
            pltpu.VMEM((COLS, 4 * C), BF16),
            pltpu.VMEM((2, SEGS, SIDE, C), BF16),
            pltpu.VMEM((2, SEGS, SIDE, C), BF16),
            pltpu.VMEM((3 * C, 3 * C), BF16),
            pltpu.VMEM((3 * C, 3 * C), BF16),
            pltpu.VMEM((C, 8 * HEAD_DIM), BF16),
            dma((16,)),
            dma((16,)),
            dma((3, 16)),
            dma((3, 16)),
            dma((2, 16)),
            dma((2, 16)),
            dma((3,)),
            dma((2, 9)),
        ],
        compiler_params=pltpu.CompilerParams(
            collective_id=0, has_side_effects=True, vmem_limit_bytes=48 * 1024 * 1024
        ),
    )(
        rotation, inverse_owner(owner), owner, counts,
        fields.reshape(SIDE * SIDE, C), w_conv1, b_conv1.reshape(1, C), w_conv2,
        b_conv2.reshape(1, C), w_query, w_key, w_value, w_out,
    )
    turned_block = pl.pallas_call(
        turn_back,
        name="turn_back",
        out_shape=jax.ShapeDtypeStruct((SIDE * SIDE, C), BF16),
        in_specs=[smem, vmem],
        out_specs=vmem,
    )(rotation, block.reshape(SIDE * SIDE, C))
    return turned_block.reshape(SIDE, SIDE, C)


def solution(mesh):
    in_specs = (P("lat", "lon", None),) + (P(),) * 11
    out_specs = P("lat", "lon", None)
    return jax.shard_map(
        on_device, mesh=mesh, in_specs=in_specs, out_specs=out_specs, check_vma=False
    )
```

```python
import functools
import math

import jax
import jax.numpy as jnp
from jax import lax
from jax.experimental import pallas as pl
from jax.experimental.pallas import tpu as pltpu
from jax.sharding import PartitionSpec as P

MESH = pl.DeviceIdType.MESH
C = 256
HEADS = 4
HEAD_DIM = 64
SIDE = 32
COLS = 512
SEGS = 16
GROUPS = 256
PIECE = 2 * SIDE
BF16 = jnp.bfloat16
F32 = jnp.float32


def row_group(lat, lon):
    pair, core = lat // 2, lat % 2
    z, high = lon // 2, lon % 2
    place = z + high * (15 - 2 * z)
    place = place + (pair % 2) * (15 - 2 * place)
    return 32 * pair + 2 * place + core


def holder(group):
    pair, rest = group // 32, group % 32
    place, core = rest // 2, rest % 2
    place = place + (pair % 2) * (15 - 2 * place)
    high = place // 8
    z = place + high * (15 - 2 * place)
    return 2 * pair + core, 2 * z + high


def turned(block, base, step_i, step_j, first, count):
    cells = lax.broadcasted_iota(jnp.int32, (count, 1), 0) + first
    source = base + step_i * (cells // SIDE) + step_j * (cells % SIDE)
    spots = lax.broadcasted_iota(jnp.int32, (count, SIDE * SIDE), 1)
    pick = jnp.where(spots == source, 1.0, 0.0).astype(BF16)
    return jnp.dot(pick, block, preferred_element_type=F32).astype(BF16)


def steps_of(quarter, upright):
    n = SIDE
    odd_a = (n * (n - 1), 1, -n)
    odd_b = (n - 1, -1, n)
    one, three = (odd_a, odd_b) if upright else (odd_b, odd_a)
    table = [(0, n, 1), one, (n * n - 1, -n, -1), three]

    def chosen(at):
        value = table[0][at]
        for k in (1, 2, 3):
            value = jnp.where(quarter == k, table[k][at], value)
        return value

    return chosen(0), chosen(1), chosen(2)


def section(
    rotation_hbm, owner_hbm, counts_hbm,
    fields_hbm, w1_hbm, b1_hbm, w2_hbm, b2_hbm,
    wq_hbm, wk_hbm, wv_hbm, wo_hbm,
    out_ref,
    rotation_ref, owner_ref, counts_ref, inverse_ref,
    fields_ref, b1_ref, b2_ref, wq_ref, wk_ref, wv_ref, wo_ref,
    upright, raw_up, raw, raw_down, rows, acts, result, outgoing, w1, w2, wkv,
    send_in, recv_in, send_halo, recv_halo, send_out, recv_out, local_sem, weight_sem,
    small_sem,
):
    lat, lon = lax.axis_index("lat"), lax.axis_index("lon")
    group = row_group(lat, lon)
    band = group // 16
    mine = band == lat
    barrier = pltpu.get_barrier_semaphore()

    def small_copies():
        pairs = (
            (rotation_hbm, rotation_ref), (fields_hbm, fields_ref),
            (owner_hbm, owner_ref), (counts_hbm, counts_ref),
            (wk_hbm, wk_ref), (wv_hbm, wv_ref),
            (b1_hbm, b1_ref), (b2_hbm, b2_ref), (wq_hbm, wq_ref), (wo_hbm, wo_ref),
        )
        for at, (source, target) in enumerate(pairs):
            yield pltpu.make_async_copy(source, target, small_sem.at[at])

    early = list(small_copies())
    for copy in early[:2]:
        copy.start()

    def greet(device):
        @pl.when(jnp.logical_or(device[0] != lat, device[1] != lon))
        def _():
            pl.semaphore_signal(barrier, inc=1, device_id=device, device_id_type=MESH)

    def greet_all(j, carry):
        greet(holder(16 * lat + j))
        greet((band, j))
        return carry

    lax.fori_loop(0, 16, greet_all, 0)

    @pl.when(group > 0)
    def _():
        pl.semaphore_signal(barrier, inc=1, device_id=holder(group - 1), device_id_type=MESH)

    @pl.when(group < GROUPS - 1)
    def _():
        pl.semaphore_signal(barrier, inc=1, device_id=holder(group + 1), device_id_type=MESH)

    def weight_copies():
        for which, (source, target) in enumerate(((w1_hbm, w1), (w2_hbm, w2))):
            for i in range(3):
                for j in range(3):
                    yield pltpu.make_async_copy(
                        source.at[i, j],
                        target.at[pl.ds(C * i, C), pl.ds(C * j, C)],
                        weight_sem.at[which, 3 * i + j],
                    )

    for copy in early[2:]:
        copy.start()
    for copy in weight_copies():
        copy.start()
    for copy in early[:2]:
        copy.wait()

    quarter = rotation_ref[lat, lon]
    base, step_i, step_j = steps_of(quarter, True)

    def turn(at, carry):
        part = turned(fields_ref[...], base, step_i, step_j, at * 256, 256)
        upright[pl.ds(4 * at, 4)] = part.reshape(4, PIECE, C)
        return carry

    lax.fori_loop(0, 4, turn, 0)

    @pl.when(group == 0)
    def _():
        raw_up[...] = jnp.zeros((SEGS, PIECE, C), BF16)

    @pl.when(group == GROUPS - 1)
    def _():
        raw_down[...] = jnp.zeros((SEGS, PIECE, C), BF16)

    for copy in early[2:6]:
        copy.wait()
    key_part = wk_ref[...]
    value_part = wv_ref[...]
    blank = jnp.zeros((HEAD_DIM, C), BF16)
    wkv[...] = jnp.concatenate(
        [key_part, blank, blank, key_part, value_part, blank, blank, value_part], axis=0
    ).T

    def invert(t, carry):
        for slot in range(3):
            from_band = jnp.clip(group - 1 + slot, 0, GROUPS - 1) // 16
            terms = [
                jnp.where(owner_ref[from_band, s] == t, s, 0) for s in range(1, SEGS)
            ]
            while len(terms) > 1:
                terms = [
                    terms[k] + terms[k + 1] if k + 1 < len(terms) else terms[k]
                    for k in range(0, len(terms), 2)
                ]
            inverse_ref[slot, t] = jnp.minimum(terms[0], SEGS - 1)
        return carry


    own = jnp.where(mine, 1, 0)
    pl.semaphore_wait(
        barrier,
        2 * (16 - own) + jnp.where(group > 0, 1, 0) + jnp.where(group < GROUPS - 1, 1, 0),
    )

    def piece_copy(j):
        return pltpu.make_async_remote_copy(
            src_ref=upright.at[j],
            dst_ref=raw.at[lon],
            send_sem=send_in.at[j],
            recv_sem=recv_in.at[lon],
            device_id=holder(16 * lat + j),
            device_id_type=MESH,
        )

    def own_copy():
        return pltpu.make_async_copy(upright.at[group % 16], raw.at[lon], local_sem.at[0])

    @pl.when(mine)
    def _():
        own_copy().start()

    def send_piece(t, carry):
        j = (group + 1 + t) % 16

        @pl.when(16 * lat + j != group)
        def _():
            piece_copy(j).start()

        return carry

    lax.fori_loop(0, 16, send_piece, 0)
    lax.fori_loop(0, SEGS, invert, 0)

    def halo_copy(s, up):
        slot = 2 if up else 0
        return pltpu.make_async_remote_copy(
            src_ref=raw.at[s],
            dst_ref=(raw_down if up else raw_up).at[s],
            send_sem=send_halo.at[slot, s],
            recv_sem=recv_halo.at[slot, s],
            device_id=holder(group - 1 if up else group + 1),
            device_id_type=MESH,
        )

    def arrived(s):
        return pltpu.make_async_remote_copy(
            src_ref=upright.at[0],
            dst_ref=raw.at[s],
            send_sem=send_in.at[0],
            recv_sem=recv_in.at[s],
            device_id=(band, s),
            device_id_type=MESH,
        )

    def forward(t, carry):
        s = (lon + t) % 16
        here = jnp.logical_and(mine, s == lon)

        @pl.when(here)
        def _():
            own_copy().wait()

        @pl.when(jnp.logical_not(here))
        def _():
            arrived(s).wait_recv()

        @pl.when(group > 0)
        def _():
            halo_copy(s, True).start()

        @pl.when(group < GROUPS - 1)
        def _():
            halo_copy(s, False).start()

        return carry

    lax.fori_loop(0, 16, forward, 0)

    def place(slot):
        for t in range(SEGS):
            s = inverse_ref[slot, t]
            piece = (raw_up, raw, raw_down)[slot][s]
            for r in range(2):
                rows[pl.ds(SIDE * t, SIDE), pl.ds(C * (2 * slot + r), C)] = piece[
                    SIDE * r : SIDE * (r + 1)
                ]

    place(1)
    for copy in early[6:]:
        copy.wait()
    for copy in weight_copies():
        copy.wait()

    def wait_halo(s, carry):
        @pl.when(group < GROUPS - 1)
        def _():
            halo_copy(s, True).wait_recv()

        @pl.when(group > 0)
        def _():
            halo_copy(s, False).wait_recv()

        return carry

    lax.fori_loop(0, 16, wait_halo, 0)
    place(0)
    place(2)

    columns = lax.broadcasted_iota(jnp.int32, (COLS, 1), 0)

    def live_of(offset):
        row = 2 * group + offset
        inside = jnp.logical_and(row >= 0, row < 2 * GROUPS)
        count = jnp.where(inside, counts_ref[jnp.clip(row, 0, 2 * GROUPS - 1)], 0)
        return jnp.where(columns < count, 1.0, 0.0)

    def convolved(source, r, weight, bias_ref):
        taps = jnp.dot(
            source[:, C * r : C * (r + 3)], weight[...], preferred_element_type=F32
        )
        return (
            pltpu.roll(taps[:, :C], 1, 0)
            + taps[:, C : 2 * C]
            + pltpu.roll(taps[:, 2 * C :], COLS - 1, 0)
            + bias_ref[...]
        )

    def make_act(r):
        first = convolved(rows, r, w1, b1_ref)
        value = first / (1.0 + jnp.exp(-first))
        acts[:, C * r : C * (r + 1)] = (value * live_of(r - 1)).astype(BF16)

    scale = math.log2(math.e) / math.sqrt(HEAD_DIM)
    lanes = lax.broadcasted_iota(jnp.int32, (1, 2 * HEAD_DIM), 1)
    low = lanes < HEAD_DIM

    def make_row(r):
        live = live_of(r)
        second = convolved(acts, r, w2, b2_ref)
        grid = rows[:, C * (r + 2) : C * (r + 3)].astype(F32)
        mixed = ((grid + second) * live).astype(BF16)
        flat = mixed.astype(F32)
        mean = jnp.mean(flat * flat, axis=1, keepdims=True)
        normed = (flat * lax.rsqrt(mean + 1e-06)).astype(BF16)
        query = jnp.dot(normed, wq_ref[...], preferred_element_type=F32)
        key_val = jnp.dot(normed, wkv[...], preferred_element_type=F32)
        bias = jnp.where(live > 0, 0.0, -1e30)
        ones = jnp.broadcast_to(live, (COLS, 2 * HEAD_DIM)).astype(BF16)
        keys, values, marks = [], [], []
        for odd in range(2):
            spot = jnp.where(lanes == (0 if odd else HEAD_DIM), 1.0, 0.0)
            pair = key_val[:, 128 * odd : 128 * (odd + 1)]
            keys.append((pair + bias * spot).astype(BF16))
            pair = key_val[:, 256 + 128 * odd : 256 + 128 * (odd + 1)].astype(BF16)
            values.append(jnp.concatenate([pair, ones], axis=1))
            marks.append(spot)
        parts = []
        for h in range(HEADS):
            odd = h % 2
            pair = query[:, 128 * (h // 2) : 128 * (h // 2 + 1)]
            keep = jnp.logical_not(low) if odd else low
            head = jnp.where(keep, pair, marks[odd]).astype(BF16)
            scores = lax.dot_general(
                head, keys[odd], (((1,), (1,)), ((), ())), preferred_element_type=F32
            )
            peak = jnp.max(scores, axis=1, keepdims=True)
            weights = jnp.exp2((scores - peak) * scale).astype(BF16)
            summed = jnp.dot(weights, values[odd], preferred_element_type=F32)
            part = summed[:, :128] / summed[:, 128:]
            if odd:
                parts[-1] = parts[-1] + part
            else:
                parts.append(part)
        attended = jnp.concatenate(parts, axis=1).astype(BF16)
        update = jnp.dot(attended, wo_ref[...], preferred_element_type=F32)
        done = (mixed.astype(F32) + update * live).astype(BF16)
        result[r] = done.reshape(SEGS, SIDE, C)

    def return_copy(r, s):
        return pltpu.make_async_remote_copy(
            src_ref=outgoing.at[r, s],
            dst_ref=out_ref.at[group % 16, pl.ds(SIDE * r, SIDE)],
            send_sem=send_out.at[r, s],
            recv_sem=recv_out.at[r, group % 16],
            device_id=(band, s),
            device_id_type=MESH,
        )

    def return_own(r):
        return pltpu.make_async_copy(
            outgoing.at[r, lon],
            out_ref.at[group % 16, pl.ds(SIDE * r, SIDE)],
            local_sem.at[1 + r],
        )

    def send_row(r):
        for s in range(SEGS):
            outgoing[r, s] = result[r, owner_ref[band, s]]

        @pl.when(mine)
        def _():
            return_own(r).start()

        def send(t, carry):
            s = (lon + 1 + t) % 16

            @pl.when(jnp.logical_or(band != lat, s != lon))
            def _():
                return_copy(r, s).start()

            return carry

        lax.fori_loop(0, 16, send, 0)

    for r in range(3):
        make_act(r)
    make_row(0)
    send_row(0)
    make_act(3)
    make_row(1)
    send_row(1)

    def drain(t, carry):
        @pl.when(16 * lat + t != group)
        def _():
            piece_copy(t).wait_send()

        @pl.when(group > 0)
        def _():
            halo_copy(t, True).wait_send()

        @pl.when(group < GROUPS - 1)
        def _():
            halo_copy(t, False).wait_send()

        @pl.when(jnp.logical_or(band != lat, t != lon))
        def _():
            for r in range(2):
                return_copy(r, t).wait_send()

        @pl.when(16 * lat + t != group)
        def _():
            for r in range(2):
                pltpu.make_async_remote_copy(
                    src_ref=outgoing.at[r, 0],
                    dst_ref=out_ref.at[t, pl.ds(SIDE * r, SIDE)],
                    send_sem=send_out.at[r, 0],
                    recv_sem=recv_out.at[r, t],
                    device_id=holder(16 * lat + t),
                    device_id_type=MESH,
                ).wait_recv()

        return carry

    lax.fori_loop(0, 16, drain, 0)

    @pl.when(mine)
    def _():
        for r in range(2):
            return_own(r).wait()


def turn_back(rotation_ref, block_ref, out_ref):
    quarter = rotation_ref[lax.axis_index("lat"), lax.axis_index("lon")]
    base, step_i, step_j = steps_of(quarter, False)

    def turn(at, carry):
        out_ref[pl.ds(at * 256, 256)] = turned(
            block_ref[...], base, step_i, step_j, at * 256, 256
        )
        return carry

    lax.fori_loop(0, 4, turn, 0)


def on_device(
    fields, w_conv1, b_conv1, w_conv2, b_conv2, w_query, w_key, w_value, w_out,
    rotation, owner, counts,
):
    smem = pl.BlockSpec(memory_space=pltpu.SMEM)
    vmem = pl.BlockSpec(memory_space=pltpu.VMEM)
    hbm = pl.BlockSpec(memory_space=pltpu.HBM)
    dma = pltpu.SemaphoreType.DMA
    block = pl.pallas_call(
        section,
        name="section",
        out_shape=jax.ShapeDtypeStruct((SEGS, PIECE, C), BF16),
        in_specs=[hbm] * 12,
        out_specs=vmem,
        scratch_shapes=[
            pltpu.SMEM((16, 16), jnp.int32),
            pltpu.SMEM((16, 16), jnp.int32),
            pltpu.SMEM((2 * GROUPS,), jnp.int32),
            pltpu.SMEM((3, SEGS), jnp.int32),
            pltpu.VMEM((SIDE * SIDE, C), BF16),
            pltpu.VMEM((1, C), F32),
            pltpu.VMEM((1, C), F32),
            pltpu.VMEM((C, C), BF16),
            pltpu.VMEM((HEAD_DIM, C), BF16),
            pltpu.VMEM((HEAD_DIM, C), BF16),
            pltpu.VMEM((C, C), BF16),
            pltpu.VMEM((SEGS, PIECE, C), BF16),
            pltpu.VMEM((SEGS, PIECE, C), BF16),
            pltpu.VMEM((SEGS, PIECE, C), BF16),
            pltpu.VMEM((SEGS, PIECE, C), BF16),
            pltpu.VMEM((COLS, 6 * C), BF16),
            pltpu.VMEM((COLS, 4 * C), BF16),
            pltpu.VMEM((2, SEGS, SIDE, C), BF16),
            pltpu.VMEM((2, SEGS, SIDE, C), BF16),
            pltpu.VMEM((3 * C, 3 * C), BF16),
            pltpu.VMEM((3 * C, 3 * C), BF16),
            pltpu.VMEM((C, 8 * HEAD_DIM), BF16),
            dma((16,)),
            dma((16,)),
            dma((3, 16)),
            dma((3, 16)),
            dma((2, 16)),
            dma((2, 16)),
            dma((3,)),
            dma((2, 9)),
            dma((10,)),
        ],
        compiler_params=pltpu.CompilerParams(
            collective_id=0, has_side_effects=True, vmem_limit_bytes=67043328
        ),
    )(
        rotation, owner, counts,
        fields.reshape(SIDE * SIDE, C), w_conv1, b_conv1.reshape(1, C), w_conv2,
        b_conv2.reshape(1, C), w_query, w_key.T, w_value.T, w_out,
    )
    turned_block = pl.pallas_call(
        turn_back,
        name="turn_back",
        out_shape=jax.ShapeDtypeStruct((SIDE * SIDE, C), BF16),
        in_specs=[smem, vmem],
        out_specs=vmem,
    )(rotation, block.reshape(SIDE * SIDE, C))
    return turned_block.reshape(SIDE, SIDE, C)


def solution(mesh):
    in_specs = (P("lat", "lon", None),) + (P(),) * 11
    out_specs = P("lat", "lon", None)
    return jax.shard_map(
        on_device, mesh=mesh, in_specs=in_specs, out_specs=out_specs, check_vma=False
    )
```

```python
import functools
import math

import jax
import jax.numpy as jnp
from jax import lax
from jax.experimental import pallas as pl
from jax.experimental.pallas import tpu as pltpu
from jax.sharding import PartitionSpec as P

MESH = pl.DeviceIdType.MESH
C = 256
HEADS = 4
HEAD_DIM = 64
SIDE = 32
COLS = 512
SEGS = 16
GROUPS = 256
PIECE = 2 * SIDE
BF16 = jnp.bfloat16
F32 = jnp.float32


def row_group(lat, lon):
    pair, core = lat // 2, lat % 2
    z, high = lon // 2, lon % 2
    place = z + high * (15 - 2 * z)
    place = place + (pair % 2) * (15 - 2 * place)
    return 32 * pair + 2 * place + core


def holder(group):
    pair, rest = group // 32, group % 32
    place, core = rest // 2, rest % 2
    place = place + (pair % 2) * (15 - 2 * place)
    high = place // 8
    z = place + high * (15 - 2 * place)
    return 2 * pair + core, 2 * z + high


def turned(block, base, step_i, step_j, first, count):
    cells = lax.broadcasted_iota(jnp.int32, (count, 1), 0) + first
    source = base + step_i * (cells // SIDE) + step_j * (cells % SIDE)
    spots = lax.broadcasted_iota(jnp.int32, (count, SIDE * SIDE), 1)
    pick = jnp.where(spots == source, 1.0, 0.0).astype(BF16)
    return jnp.dot(pick, block, preferred_element_type=F32).astype(BF16)


def steps_of(quarter, upright):
    n = SIDE
    odd_a = (n * (n - 1), 1, -n)
    odd_b = (n - 1, -1, n)
    one, three = (odd_a, odd_b) if upright else (odd_b, odd_a)
    table = [(0, n, 1), one, (n * n - 1, -n, -1), three]

    def chosen(at):
        value = table[0][at]
        for k in (1, 2, 3):
            value = jnp.where(quarter == k, table[k][at], value)
        return value

    return chosen(0), chosen(1), chosen(2)


def section(
    rotation_hbm, owner_hbm, counts_hbm,
    fields_hbm, w1_hbm, b1_hbm, w2_hbm, b2_hbm,
    wq_hbm, wk_hbm, wv_hbm, wo_hbm,
    out_ref,
    rotation_ref, owner_ref, counts_ref, inverse_ref,
    fields_ref, b1_ref, b2_ref, wq_ref, wk_ref, wv_ref, wo_ref,
    upright, raw_up, raw, raw_down, rows, acts, mixed_rows, queries, outgoing, w1, w2, wkv,
    send_in, recv_in, send_halo, recv_halo, send_out, recv_out, local_sem, weight_sem,
    small_sem,
):
    lat, lon = lax.axis_index("lat"), lax.axis_index("lon")
    group = row_group(lat, lon)
    band = group // 16
    mine = band == lat
    barrier = pltpu.get_barrier_semaphore()

    def small_copies():
        pairs = (
            (rotation_hbm, rotation_ref), (fields_hbm, fields_ref),
            (owner_hbm, owner_ref), (counts_hbm, counts_ref),
            (wk_hbm, wk_ref), (wv_hbm, wv_ref),
            (b1_hbm, b1_ref), (b2_hbm, b2_ref), (wq_hbm, wq_ref), (wo_hbm, wo_ref),
        )
        for at, (source, target) in enumerate(pairs):
            yield pltpu.make_async_copy(source, target, small_sem.at[at])

    early = list(small_copies())
    for copy in early[:2]:
        copy.start()

    def greet(device):
        @pl.when(jnp.logical_or(device[0] != lat, device[1] != lon))
        def _():
            pl.semaphore_signal(barrier, inc=1, device_id=device, device_id_type=MESH)

    def greet_all(j, carry):
        greet(holder(16 * lat + j))
        greet((band, j))
        return carry

    lax.fori_loop(0, 16, greet_all, 0)

    @pl.when(group > 0)
    def _():
        pl.semaphore_signal(barrier, inc=1, device_id=holder(group - 1), device_id_type=MESH)

    @pl.when(group < GROUPS - 1)
    def _():
        pl.semaphore_signal(barrier, inc=1, device_id=holder(group + 1), device_id_type=MESH)

    def weight_copies():
        for which, (source, target) in enumerate(((w1_hbm, w1), (w2_hbm, w2))):
            for i in range(3):
                for j in range(3):
                    yield pltpu.make_async_copy(
                        source.at[i, j],
                        target.at[pl.ds(C * i, C), pl.ds(C * j, C)],
                        weight_sem.at[which, 3 * i + j],
                    )

    for copy in early[2:]:
        copy.start()
    for copy in weight_copies():
        copy.start()
    for copy in early[:2]:
        copy.wait()

    quarter = rotation_ref[lat, lon]
    base, step_i, step_j = steps_of(quarter, True)

    def turn(at, carry):
        part = turned(fields_ref[...], base, step_i, step_j, at * 256, 256)
        upright[pl.ds(4 * at, 4)] = part.reshape(4, PIECE, C)
        return carry

    lax.fori_loop(0, 4, turn, 0)

    @pl.when(group == 0)
    def _():
        raw_up[...] = jnp.zeros((SEGS, PIECE, C), BF16)

    @pl.when(group == GROUPS - 1)
    def _():
        raw_down[...] = jnp.zeros((SEGS, PIECE, C), BF16)

    for copy in early[2:6]:
        copy.wait()
    key_part = wk_ref[...]
    value_part = wv_ref[...]
    blank = jnp.zeros((HEAD_DIM, C), BF16)
    wkv[...] = jnp.concatenate(
        [key_part, blank, blank, key_part, value_part, blank, blank, value_part], axis=0
    ).T

    def invert(t, carry):
        for slot in range(3):
            from_band = jnp.clip(group - 1 + slot, 0, GROUPS - 1) // 16
            terms = [
                jnp.where(owner_ref[from_band, s] == t, s, 0) for s in range(1, SEGS)
            ]
            while len(terms) > 1:
                terms = [
                    terms[k] + terms[k + 1] if k + 1 < len(terms) else terms[k]
                    for k in range(0, len(terms), 2)
                ]
            inverse_ref[slot, t] = jnp.minimum(terms[0], SEGS - 1)
        return carry


    own = jnp.where(mine, 1, 0)
    pl.semaphore_wait(
        barrier,
        2 * (16 - own) + jnp.where(group > 0, 1, 0) + jnp.where(group < GROUPS - 1, 1, 0),
    )

    def piece_copy(j):
        return pltpu.make_async_remote_copy(
            src_ref=upright.at[j],
            dst_ref=raw.at[lon],
            send_sem=send_in.at[j],
            recv_sem=recv_in.at[lon],
            device_id=holder(16 * lat + j),
            device_id_type=MESH,
        )

    def own_copy():
        return pltpu.make_async_copy(upright.at[group % 16], raw.at[lon], local_sem.at[0])

    @pl.when(mine)
    def _():
        own_copy().start()

    def send_piece(t, carry):
        j = (group + 1 + t) % 16

        @pl.when(16 * lat + j != group)
        def _():
            piece_copy(j).start()

        return carry

    lax.fori_loop(0, 16, send_piece, 0)
    lax.fori_loop(0, SEGS, invert, 0)

    def halo_copy(s, up):
        slot = 2 if up else 0
        return pltpu.make_async_remote_copy(
            src_ref=raw.at[s],
            dst_ref=(raw_down if up else raw_up).at[s],
            send_sem=send_halo.at[slot, s],
            recv_sem=recv_halo.at[slot, s],
            device_id=holder(group - 1 if up else group + 1),
            device_id_type=MESH,
        )

    def arrived(s):
        return pltpu.make_async_remote_copy(
            src_ref=upright.at[0],
            dst_ref=raw.at[s],
            send_sem=send_in.at[0],
            recv_sem=recv_in.at[s],
            device_id=(band, s),
            device_id_type=MESH,
        )

    def forward(t, carry):
        s = (lon + t) % 16
        here = jnp.logical_and(mine, s == lon)

        @pl.when(here)
        def _():
            own_copy().wait()

        @pl.when(jnp.logical_not(here))
        def _():
            arrived(s).wait_recv()

        @pl.when(group > 0)
        def _():
            halo_copy(s, True).start()

        @pl.when(group < GROUPS - 1)
        def _():
            halo_copy(s, False).start()

        return carry

    lax.fori_loop(0, 16, forward, 0)

    def place(slot):
        for t in range(SEGS):
            s = inverse_ref[slot, t]
            piece = (raw_up, raw, raw_down)[slot][s]
            for r in range(2):
                rows[pl.ds(SIDE * t, SIDE), pl.ds(C * (2 * slot + r), C)] = piece[
                    SIDE * r : SIDE * (r + 1)
                ]

    place(1)
    for copy in early[6:]:
        copy.wait()
    for copy in weight_copies():
        copy.wait()

    def wait_halo(s, carry):
        @pl.when(group < GROUPS - 1)
        def _():
            halo_copy(s, True).wait_recv()

        @pl.when(group > 0)
        def _():
            halo_copy(s, False).wait_recv()

        return carry

    lax.fori_loop(0, 16, wait_halo, 0)
    place(0)
    place(2)

    columns = lax.broadcasted_iota(jnp.int32, (COLS, 1), 0)

    def live_of(offset):
        row = 2 * group + offset
        inside = jnp.logical_and(row >= 0, row < 2 * GROUPS)
        count = jnp.where(inside, counts_ref[jnp.clip(row, 0, 2 * GROUPS - 1)], 0)
        return jnp.where(columns < count, 1.0, 0.0)

    def convolved(source, r, weight, bias_ref):
        taps = jnp.dot(
            source[:, C * r : C * (r + 3)], weight[...], preferred_element_type=F32
        )
        return (
            pltpu.roll(taps[:, :C], 1, 0)
            + taps[:, C : 2 * C]
            + pltpu.roll(taps[:, 2 * C :], COLS - 1, 0)
            + bias_ref[...]
        )

    def make_act(r):
        first = convolved(rows, r, w1, b1_ref)
        value = first / (1.0 + jnp.exp(-first))
        acts[:, C * r : C * (r + 1)] = (value * live_of(r - 1)).astype(BF16)

    scale = math.log2(math.e) / math.sqrt(HEAD_DIM)
    lanes = lax.broadcasted_iota(jnp.int32, (1, 2 * HEAD_DIM), 1)
    low = lanes < HEAD_DIM
    marks = [
        jnp.where(lanes == (0 if odd else HEAD_DIM), 1.0, 0.0) for odd in range(2)
    ]

    def make_row(r):
        live = live_of(r)
        second = convolved(acts, r, w2, b2_ref)
        grid = rows[:, C * (r + 2) : C * (r + 3)].astype(F32)
        mixed = ((grid + second) * live).astype(BF16)
        flat = mixed.astype(F32)
        mean = jnp.mean(flat * flat, axis=1, keepdims=True)
        normed = (flat * lax.rsqrt(mean + 1e-06)).astype(BF16)
        query = jnp.dot(normed, wq_ref[...], preferred_element_type=F32)
        mixed_rows[r] = mixed.reshape(SEGS, SIDE, C)
        queries[r] = query.astype(BF16).reshape(SEGS, SIDE, C)
        key_val = jnp.dot(normed, wkv[...], preferred_element_type=F32)
        bias = jnp.where(live > 0, 0.0, -1e30)
        ones = jnp.broadcast_to(live, (COLS, 2 * HEAD_DIM)).astype(BF16)
        keys, values = [], []
        for odd in range(2):
            pair = key_val[:, 128 * odd : 128 * (odd + 1)]
            keys.append((pair + bias * marks[odd]).astype(BF16))
            pair = key_val[:, 256 + 128 * odd : 256 + 128 * (odd + 1)].astype(BF16)
            values.append(jnp.concatenate([pair, ones], axis=1))
        count = counts_ref[2 * group + r]
        for offsets in ((3, 5), (4, 0), (2, 6), (1, 7)):
            shards = [
                2 * ((lon // 2 + offset) % 8) + high for offset in offsets for high in range(2)
            ]
            make_chunk(r, shards, count, keys, values)

    cells = lax.broadcasted_iota(jnp.int32, (SIDE, 1), 0)

    def make_chunk(r, shards, count, keys, values):
        segs = [owner_ref[band, s] for s in shards]
        query = jnp.concatenate([queries[r, t] for t in segs], axis=0)
        mixed = jnp.concatenate([mixed_rows[r, t] for t in segs], axis=0)
        live = jnp.concatenate(
            [jnp.where(cells + SIDE * t < count, 1.0, 0.0) for t in segs], axis=0
        )
        size = 4 * SIDE
        halves = []
        for odd in range(2):
            keep = jnp.logical_not(low) if odd else low
            heads = jnp.concatenate([query[:, :128], query[:, 128:]], axis=0)
            heads = jnp.where(keep, heads, marks[odd].astype(BF16))
            scores = lax.dot_general(
                heads, keys[odd], (((1,), (1,)), ((), ())), preferred_element_type=F32
            )
            peak = jnp.max(scores, axis=1, keepdims=True)
            weights = jnp.exp2((scores - peak) * scale).astype(BF16)
            summed = jnp.dot(weights, values[odd], preferred_element_type=F32)
            halves.append(summed[:, :128] / summed[:, 128:])
        both = halves[0] + halves[1]
        attended = jnp.concatenate([both[:size], both[size:]], axis=1).astype(BF16)
        update = jnp.dot(attended, wo_ref[...], preferred_element_type=F32)
        done = (mixed.astype(F32) + update * live).astype(BF16).reshape(4, SIDE, C)
        for k, s in enumerate(shards):
            outgoing[r, s] = done[k]
        for s in shards:
            here = jnp.logical_and(mine, s == lon)

            @pl.when(here)
            def _():
                return_own(r).start()

            @pl.when(jnp.logical_not(here))
            def _():
                return_copy(r, s).start()

    def return_copy(r, s):
        return pltpu.make_async_remote_copy(
            src_ref=outgoing.at[r, s],
            dst_ref=out_ref.at[group % 16, pl.ds(SIDE * r, SIDE)],
            send_sem=send_out.at[r, s],
            recv_sem=recv_out.at[r, group % 16],
            device_id=(band, s),
            device_id_type=MESH,
        )

    def return_own(r):
        return pltpu.make_async_copy(
            outgoing.at[r, lon],
            out_ref.at[group % 16, pl.ds(SIDE * r, SIDE)],
            local_sem.at[1 + r],
        )

    for r in range(3):
        make_act(r)
    make_row(0)
    make_act(3)
    make_row(1)

    def drain(t, carry):
        @pl.when(16 * lat + t != group)
        def _():
            piece_copy(t).wait_send()

        @pl.when(group > 0)
        def _():
            halo_copy(t, True).wait_send()

        @pl.when(group < GROUPS - 1)
        def _():
            halo_copy(t, False).wait_send()

        @pl.when(jnp.logical_or(band != lat, t != lon))
        def _():
            for r in range(2):
                return_copy(r, t).wait_send()

        @pl.when(16 * lat + t != group)
        def _():
            for r in range(2):
                pltpu.make_async_remote_copy(
                    src_ref=outgoing.at[r, 0],
                    dst_ref=out_ref.at[t, pl.ds(SIDE * r, SIDE)],
                    send_sem=send_out.at[r, 0],
                    recv_sem=recv_out.at[r, t],
                    device_id=holder(16 * lat + t),
                    device_id_type=MESH,
                ).wait_recv()

        return carry

    lax.fori_loop(0, 16, drain, 0)

    @pl.when(mine)
    def _():
        for r in range(2):
            return_own(r).wait()


def turn_back(rotation_ref, block_ref, out_ref):
    quarter = rotation_ref[lax.axis_index("lat"), lax.axis_index("lon")]
    base, step_i, step_j = steps_of(quarter, False)

    def turn(at, carry):
        out_ref[pl.ds(at * 256, 256)] = turned(
            block_ref[...], base, step_i, step_j, at * 256, 256
        )
        return carry

    lax.fori_loop(0, 4, turn, 0)


def on_device(
    fields, w_conv1, b_conv1, w_conv2, b_conv2, w_query, w_key, w_value, w_out,
    rotation, owner, counts,
):
    smem = pl.BlockSpec(memory_space=pltpu.SMEM)
    vmem = pl.BlockSpec(memory_space=pltpu.VMEM)
    hbm = pl.BlockSpec(memory_space=pltpu.HBM)
    dma = pltpu.SemaphoreType.DMA
    block = pl.pallas_call(
        section,
        name="section",
        out_shape=jax.ShapeDtypeStruct((SEGS, PIECE, C), BF16),
        in_specs=[hbm] * 12,
        out_specs=vmem,
        scratch_shapes=[
            pltpu.SMEM((16, 16), jnp.int32),
            pltpu.SMEM((16, 16), jnp.int32),
            pltpu.SMEM((2 * GROUPS,), jnp.int32),
            pltpu.SMEM((3, SEGS), jnp.int32),
            pltpu.VMEM((SIDE * SIDE, C), BF16),
            pltpu.VMEM((1, C), F32),
            pltpu.VMEM((1, C), F32),
            pltpu.VMEM((C, C), BF16),
            pltpu.VMEM((HEAD_DIM, C), BF16),
            pltpu.VMEM((HEAD_DIM, C), BF16),
            pltpu.VMEM((C, C), BF16),
            pltpu.VMEM((SEGS, PIECE, C), BF16),
            pltpu.VMEM((SEGS, PIECE, C), BF16),
            pltpu.VMEM((SEGS, PIECE, C), BF16),
            pltpu.VMEM((SEGS, PIECE, C), BF16),
            pltpu.VMEM((COLS, 6 * C), BF16),
            pltpu.VMEM((COLS, 4 * C), BF16),
            pltpu.VMEM((2, SEGS, SIDE, C), BF16),
            pltpu.VMEM((2, SEGS, SIDE, C), BF16),
            pltpu.VMEM((2, SEGS, SIDE, C), BF16),
            pltpu.VMEM((3 * C, 3 * C), BF16),
            pltpu.VMEM((3 * C, 3 * C), BF16),
            pltpu.VMEM((C, 8 * HEAD_DIM), BF16),
            dma((16,)),
            dma((16,)),
            dma((3, 16)),
            dma((3, 16)),
            dma((2, 16)),
            dma((2, 16)),
            dma((3,)),
            dma((2, 9)),
            dma((10,)),
        ],
        compiler_params=pltpu.CompilerParams(
            collective_id=0, has_side_effects=True, vmem_limit_bytes=67043328
        ),
    )(
        rotation, owner, counts,
        fields.reshape(SIDE * SIDE, C), w_conv1, b_conv1.reshape(1, C), w_conv2,
        b_conv2.reshape(1, C), w_query, w_key.T, w_value.T, w_out,
    )
    turned_block = pl.pallas_call(
        turn_back,
        name="turn_back",
        out_shape=jax.ShapeDtypeStruct((SIDE * SIDE, C), BF16),
        in_specs=[smem, vmem],
        out_specs=vmem,
    )(rotation, block.reshape(SIDE * SIDE, C))
    return turned_block.reshape(SIDE, SIDE, C)


def solution(mesh):
    in_specs = (P("lat", "lon", None),) + (P(),) * 11
    out_specs = P("lat", "lon", None)
    return jax.shard_map(
        on_device, mesh=mesh, in_specs=in_specs, out_specs=out_specs, check_vma=False
    )
```

```python
import functools
import math

import jax
import jax.numpy as jnp
from jax import lax
from jax.experimental import pallas as pl
from jax.experimental.pallas import tpu as pltpu
from jax.sharding import PartitionSpec as P

MESH = pl.DeviceIdType.MESH
C = 256
HEADS = 4
HEAD_DIM = 64
SIDE = 32
COLS = 512
SEGS = 16
GROUPS = 256
PIECE = 2 * SIDE
BF16 = jnp.bfloat16
F32 = jnp.float32


def row_group(lat, lon):
    pair, core = lat // 2, lat % 2
    z, high = lon // 2, lon % 2
    place = z + high * (15 - 2 * z)
    place = place + (pair % 2) * (15 - 2 * place)
    return 32 * pair + 2 * place + core


def holder(group):
    pair, rest = group // 32, group % 32
    place, core = rest // 2, rest % 2
    place = place + (pair % 2) * (15 - 2 * place)
    high = place // 8
    z = place + high * (15 - 2 * place)
    return 2 * pair + core, 2 * z + high


def turned(block, base, step_i, step_j, first, count):
    cells = lax.broadcasted_iota(jnp.int32, (count, 1), 0) + first
    source = base + step_i * (cells // SIDE) + step_j * (cells % SIDE)
    spots = lax.broadcasted_iota(jnp.int32, (count, SIDE * SIDE), 1)
    pick = jnp.where(spots == source, 1.0, 0.0).astype(BF16)
    return jnp.dot(pick, block, preferred_element_type=F32).astype(BF16)


def steps_of(quarter, upright):
    n = SIDE
    odd_a = (n * (n - 1), 1, -n)
    odd_b = (n - 1, -1, n)
    one, three = (odd_a, odd_b) if upright else (odd_b, odd_a)
    table = [(0, n, 1), one, (n * n - 1, -n, -1), three]

    def chosen(at):
        value = table[0][at]
        for k in (1, 2, 3):
            value = jnp.where(quarter == k, table[k][at], value)
        return value

    return chosen(0), chosen(1), chosen(2)


def section(
    rotation_hbm, owner_hbm, counts_hbm,
    fields_hbm, w1_hbm, b1_hbm, w2_hbm, b2_hbm,
    wq_hbm, wk_hbm, wv_hbm, wo_hbm,
    out_ref,
    rotation_ref, owner_ref, counts_ref, inverse_ref,
    fields_ref, b1_ref, b2_ref, wq_ref, wk_ref, wv_ref, wo_ref,
    upright, raw_up, raw, raw_down, rows, acts, mixed_rows, queries, outgoing, w1, w2, wkv,
    send_in, recv_in, send_halo, recv_halo, send_out, recv_out, local_sem, weight_sem,
    small_sem, partial,
):
    lat, lon = lax.axis_index("lat"), lax.axis_index("lon")
    group = row_group(lat, lon)
    band = group // 16
    mine = band == lat
    barrier = pltpu.get_barrier_semaphore()

    def small_copies():
        pairs = (
            (rotation_hbm, rotation_ref), (fields_hbm, fields_ref),
            (owner_hbm, owner_ref), (counts_hbm, counts_ref),
            (wk_hbm, wk_ref), (wv_hbm, wv_ref),
            (b1_hbm, b1_ref), (b2_hbm, b2_ref), (wq_hbm, wq_ref), (wo_hbm, wo_ref),
        )
        for at, (source, target) in enumerate(pairs):
            yield pltpu.make_async_copy(source, target, small_sem.at[at])

    early = list(small_copies())
    for copy in early[:2]:
        copy.start()

    def greet(device):
        @pl.when(jnp.logical_or(device[0] != lat, device[1] != lon))
        def _():
            pl.semaphore_signal(barrier, inc=1, device_id=device, device_id_type=MESH)

    def greet_all(j, carry):
        greet(holder(16 * lat + j))
        greet((band, j))
        return carry

    lax.fori_loop(0, 16, greet_all, 0)

    @pl.when(group > 0)
    def _():
        pl.semaphore_signal(barrier, inc=1, device_id=holder(group - 1), device_id_type=MESH)

    @pl.when(group < GROUPS - 1)
    def _():
        pl.semaphore_signal(barrier, inc=1, device_id=holder(group + 1), device_id_type=MESH)

    def weight_copies():
        for which, (source, target) in enumerate(((w1_hbm, w1), (w2_hbm, w2))):
            for i in range(3):
                for j in range(3):
                    yield pltpu.make_async_copy(
                        source.at[i, j],
                        target.at[pl.ds(C * i, C), pl.ds(C * j, C)],
                        weight_sem.at[which, 3 * i + j],
                    )

    for copy in early[2:]:
        copy.start()
    for copy in weight_copies():
        copy.start()
    for copy in early[:2]:
        copy.wait()

    quarter = rotation_ref[lat, lon]
    base, step_i, step_j = steps_of(quarter, True)

    def turn(at, carry):
        part = turned(fields_ref[...], base, step_i, step_j, at * 256, 256)
        upright[pl.ds(4 * at, 4)] = part.reshape(4, PIECE, C)
        return carry

    lax.fori_loop(0, 4, turn, 0)

    @pl.when(group == 0)
    def _():
        raw_up[...] = jnp.zeros((SEGS, PIECE, C), BF16)

    @pl.when(group == GROUPS - 1)
    def _():
        raw_down[...] = jnp.zeros((SEGS, PIECE, C), BF16)

    for copy in early[2:6]:
        copy.wait()
    key_part = wk_ref[...]
    value_part = wv_ref[...]
    blank = jnp.zeros((HEAD_DIM, C), BF16)
    wkv[...] = jnp.concatenate(
        [key_part, blank, blank, key_part, value_part, blank, blank, value_part], axis=0
    ).T

    def invert(t, carry):
        for slot in range(3):
            from_band = jnp.clip(group - 1 + slot, 0, GROUPS - 1) // 16
            terms = [
                jnp.where(owner_ref[from_band, s] == t, s, 0) for s in range(1, SEGS)
            ]
            while len(terms) > 1:
                terms = [
                    terms[k] + terms[k + 1] if k + 1 < len(terms) else terms[k]
                    for k in range(0, len(terms), 2)
                ]
            inverse_ref[slot, t] = jnp.minimum(terms[0], SEGS - 1)
        return carry


    own = jnp.where(mine, 1, 0)
    pl.semaphore_wait(
        barrier,
        2 * (16 - own) + jnp.where(group > 0, 1, 0) + jnp.where(group < GROUPS - 1, 1, 0),
    )

    def piece_copy(j):
        return pltpu.make_async_remote_copy(
            src_ref=upright.at[j],
            dst_ref=raw.at[lon],
            send_sem=send_in.at[j],
            recv_sem=recv_in.at[lon],
            device_id=holder(16 * lat + j),
            device_id_type=MESH,
        )

    def own_copy():
        return pltpu.make_async_copy(upright.at[group % 16], raw.at[lon], local_sem.at[0])

    @pl.when(mine)
    def _():
        own_copy().start()

    def send_piece(t, carry):
        j = (group + 1 + t) % 16

        @pl.when(16 * lat + j != group)
        def _():
            piece_copy(j).start()

        return carry

    lax.fori_loop(0, 16, send_piece, 0)
    lax.fori_loop(0, SEGS, invert, 0)

    def halo_copy(s, up):
        slot = 2 if up else 0
        return pltpu.make_async_remote_copy(
            src_ref=raw.at[s],
            dst_ref=(raw_down if up else raw_up).at[s],
            send_sem=send_halo.at[slot, s],
            recv_sem=recv_halo.at[slot, s],
            device_id=holder(group - 1 if up else group + 1),
            device_id_type=MESH,
        )

    def arrived(s):
        return pltpu.make_async_remote_copy(
            src_ref=upright.at[0],
            dst_ref=raw.at[s],
            send_sem=send_in.at[0],
            recv_sem=recv_in.at[s],
            device_id=(band, s),
            device_id_type=MESH,
        )

    def forward(t, carry):
        s = (lon + t) % 16
        here = jnp.logical_and(mine, s == lon)

        @pl.when(here)
        def _():
            own_copy().wait()

        @pl.when(jnp.logical_not(here))
        def _():
            arrived(s).wait_recv()

        @pl.when(group > 0)
        def _():
            halo_copy(s, True).start()

        @pl.when(group < GROUPS - 1)
        def _():
            halo_copy(s, False).start()

        return carry

    lax.fori_loop(0, 16, forward, 0)

    def place(slot):
        for t in range(SEGS):
            s = inverse_ref[slot, t]
            piece = (raw_up, raw, raw_down)[slot][s]
            for r in range(2):
                rows[pl.ds(SIDE * t, SIDE), pl.ds(C * (2 * slot + r), C)] = piece[
                    SIDE * r : SIDE * (r + 1)
                ]

    place(1)
    for copy in early[6:]:
        copy.wait()
    for copy in weight_copies():
        copy.wait()

    def mixed_taps(source, r, weight, low_tap, high_tap):
        taps = jnp.dot(
            source[:, C * (r + low_tap) : C * (r + high_tap)],
            weight[C * low_tap : C * high_tap],
            preferred_element_type=F32,
        )
        return (
            pltpu.roll(taps[:, :C], 1, 0)
            + taps[:, C : 2 * C]
            + pltpu.roll(taps[:, 2 * C :], COLS - 1, 0)
        )

    for r, (low_tap, high_tap) in enumerate(((2, 3), (1, 3), (0, 2), (0, 1))):
        partial[r] = mixed_taps(rows, r, w1, low_tap, high_tap) + b1_ref[...]

    def wait_halo(s, carry):
        @pl.when(group < GROUPS - 1)
        def _():
            halo_copy(s, True).wait_recv()

        @pl.when(group > 0)
        def _():
            halo_copy(s, False).wait_recv()

        return carry

    lax.fori_loop(0, 16, wait_halo, 0)
    place(0)
    place(2)

    columns = lax.broadcasted_iota(jnp.int32, (COLS, 1), 0)

    def live_of(offset):
        row = 2 * group + offset
        inside = jnp.logical_and(row >= 0, row < 2 * GROUPS)
        count = jnp.where(inside, counts_ref[jnp.clip(row, 0, 2 * GROUPS - 1)], 0)
        return jnp.where(columns < count, 1.0, 0.0)

    def make_act(r):
        low_tap, high_tap = ((0, 2), (0, 1), (2, 3), (1, 3))[r]
        first = mixed_taps(rows, r, w1, low_tap, high_tap) + partial[r]
        value = first / (1.0 + jnp.exp(-first))
        acts[:, C * r : C * (r + 1)] = (value * live_of(r - 1)).astype(BF16)

    scale = math.log2(math.e) / math.sqrt(HEAD_DIM)
    lanes = lax.broadcasted_iota(jnp.int32, (1, 2 * HEAD_DIM), 1)
    low = lanes < HEAD_DIM
    marks = [
        jnp.where(lanes == (0 if odd else HEAD_DIM), 1.0, 0.0) for odd in range(2)
    ]

    def make_row(r):
        live = live_of(r)
        second = mixed_taps(acts, r, w2, 0, 3) + b2_ref[...]
        grid = rows[:, C * (r + 2) : C * (r + 3)].astype(F32)
        mixed = ((grid + second) * live).astype(BF16)
        flat = mixed.astype(F32)
        mean = jnp.mean(flat * flat, axis=1, keepdims=True)
        normed = (flat * lax.rsqrt(mean + 1e-06)).astype(BF16)
        query = jnp.dot(normed, wq_ref[...], preferred_element_type=F32)
        mixed_rows[r] = mixed.reshape(SEGS, SIDE, C)
        queries[r] = query.astype(BF16).reshape(SEGS, SIDE, C)
        key_val = jnp.dot(normed, wkv[...], preferred_element_type=F32)
        bias = jnp.where(live > 0, 0.0, -1e30)
        ones = jnp.broadcast_to(live, (COLS, 2 * HEAD_DIM)).astype(BF16)
        keys, values = [], []
        for odd in range(2):
            pair = key_val[:, 128 * odd : 128 * (odd + 1)]
            keys.append((pair + bias * marks[odd]).astype(BF16))
            pair = key_val[:, 256 + 128 * odd : 256 + 128 * (odd + 1)].astype(BF16)
            values.append(jnp.concatenate([pair, ones], axis=1))
        count = counts_ref[2 * group + r]
        for offsets in ((3, 5), (4, 0), (2, 6), (1, 7)):
            shards = [
                2 * ((lon // 2 + offset) % 8) + high for offset in offsets for high in range(2)
            ]
            make_chunk(r, shards, count, keys, values)

    cells = lax.broadcasted_iota(jnp.int32, (SIDE, 1), 0)

    def make_chunk(r, shards, count, keys, values):
        segs = [owner_ref[band, s] for s in shards]
        query = jnp.concatenate([queries[r, t] for t in segs], axis=0)
        mixed = jnp.concatenate([mixed_rows[r, t] for t in segs], axis=0)
        live = jnp.concatenate(
            [jnp.where(cells + SIDE * t < count, 1.0, 0.0) for t in segs], axis=0
        )
        size = 4 * SIDE
        halves = []
        for odd in range(2):
            keep = jnp.logical_not(low) if odd else low
            heads = jnp.concatenate([query[:, :128], query[:, 128:]], axis=0)
            heads = jnp.where(keep, heads, marks[odd].astype(BF16))
            scores = lax.dot_general(
                heads, keys[odd], (((1,), (1,)), ((), ())), preferred_element_type=F32
            )
            peak = jnp.max(scores, axis=1, keepdims=True)
            weights = jnp.exp2((scores - peak) * scale).astype(BF16)
            summed = jnp.dot(weights, values[odd], preferred_element_type=F32)
            halves.append(summed[:, :128] / summed[:, 128:])
        both = halves[0] + halves[1]
        attended = jnp.concatenate([both[:size], both[size:]], axis=1).astype(BF16)
        update = jnp.dot(attended, wo_ref[...], preferred_element_type=F32)
        done = (mixed.astype(F32) + update * live).astype(BF16).reshape(4, SIDE, C)
        for k, s in enumerate(shards):
            outgoing[r, s] = done[k]
        for s in shards:
            here = jnp.logical_and(mine, s == lon)

            @pl.when(here)
            def _():
                return_own(r).start()

            @pl.when(jnp.logical_not(here))
            def _():
                return_copy(r, s).start()

    def return_copy(r, s):
        return pltpu.make_async_remote_copy(
            src_ref=outgoing.at[r, s],
            dst_ref=out_ref.at[group % 16, pl.ds(SIDE * r, SIDE)],
            send_sem=send_out.at[r, s],
            recv_sem=recv_out.at[r, group % 16],
            device_id=(band, s),
            device_id_type=MESH,
        )

    def return_own(r):
        return pltpu.make_async_copy(
            outgoing.at[r, lon],
            out_ref.at[group % 16, pl.ds(SIDE * r, SIDE)],
            local_sem.at[1 + r],
        )

    for r in range(3):
        make_act(r)
    make_row(0)
    make_act(3)
    make_row(1)

    def drain(t, carry):
        @pl.when(16 * lat + t != group)
        def _():
            piece_copy(t).wait_send()

        @pl.when(group > 0)
        def _():
            halo_copy(t, True).wait_send()

        @pl.when(group < GROUPS - 1)
        def _():
            halo_copy(t, False).wait_send()

        @pl.when(jnp.logical_or(band != lat, t != lon))
        def _():
            for r in range(2):
                return_copy(r, t).wait_send()

        @pl.when(16 * lat + t != group)
        def _():
            for r in range(2):
                pltpu.make_async_remote_copy(
                    src_ref=outgoing.at[r, 0],
                    dst_ref=out_ref.at[t, pl.ds(SIDE * r, SIDE)],
                    send_sem=send_out.at[r, 0],
                    recv_sem=recv_out.at[r, t],
                    device_id=holder(16 * lat + t),
                    device_id_type=MESH,
                ).wait_recv()

        return carry

    lax.fori_loop(0, 16, drain, 0)

    @pl.when(mine)
    def _():
        for r in range(2):
            return_own(r).wait()


def turn_back(rotation_ref, block_ref, out_ref):
    quarter = rotation_ref[lax.axis_index("lat"), lax.axis_index("lon")]
    base, step_i, step_j = steps_of(quarter, False)

    def turn(at, carry):
        out_ref[pl.ds(at * 256, 256)] = turned(
            block_ref[...], base, step_i, step_j, at * 256, 256
        )
        return carry

    lax.fori_loop(0, 4, turn, 0)


def on_device(
    fields, w_conv1, b_conv1, w_conv2, b_conv2, w_query, w_key, w_value, w_out,
    rotation, owner, counts,
):
    smem = pl.BlockSpec(memory_space=pltpu.SMEM)
    vmem = pl.BlockSpec(memory_space=pltpu.VMEM)
    hbm = pl.BlockSpec(memory_space=pltpu.HBM)
    dma = pltpu.SemaphoreType.DMA
    block = pl.pallas_call(
        section,
        name="section",
        out_shape=jax.ShapeDtypeStruct((SEGS, PIECE, C), BF16),
        in_specs=[hbm] * 12,
        out_specs=vmem,
        scratch_shapes=[
            pltpu.SMEM((16, 16), jnp.int32),
            pltpu.SMEM((16, 16), jnp.int32),
            pltpu.SMEM((2 * GROUPS,), jnp.int32),
            pltpu.SMEM((3, SEGS), jnp.int32),
            pltpu.VMEM((SIDE * SIDE, C), BF16),
            pltpu.VMEM((1, C), F32),
            pltpu.VMEM((1, C), F32),
            pltpu.VMEM((C, C), BF16),
            pltpu.VMEM((HEAD_DIM, C), BF16),
            pltpu.VMEM((HEAD_DIM, C), BF16),
            pltpu.VMEM((C, C), BF16),
            pltpu.VMEM((SEGS, PIECE, C), BF16),
            pltpu.VMEM((SEGS, PIECE, C), BF16),
            pltpu.VMEM((SEGS, PIECE, C), BF16),
            pltpu.VMEM((SEGS, PIECE, C), BF16),
            pltpu.VMEM((COLS, 6 * C), BF16),
            pltpu.VMEM((COLS, 4 * C), BF16),
            pltpu.VMEM((2, SEGS, SIDE, C), BF16),
            pltpu.VMEM((2, SEGS, SIDE, C), BF16),
            pltpu.VMEM((2, SEGS, SIDE, C), BF16),
            pltpu.VMEM((3 * C, 3 * C), BF16),
            pltpu.VMEM((3 * C, 3 * C), BF16),
            pltpu.VMEM((C, 8 * HEAD_DIM), BF16),
            dma((16,)),
            dma((16,)),
            dma((3, 16)),
            dma((3, 16)),
            dma((2, 16)),
            dma((2, 16)),
            dma((3,)),
            dma((2, 9)),
            dma((10,)),
            pltpu.VMEM((4, COLS, C), F32),
        ],
        compiler_params=pltpu.CompilerParams(
            collective_id=0, has_side_effects=True, vmem_limit_bytes=67043328
        ),
    )(
        rotation, owner, counts,
        fields.reshape(SIDE * SIDE, C), w_conv1, b_conv1.reshape(1, C), w_conv2,
        b_conv2.reshape(1, C), w_query, w_key.T, w_value.T, w_out,
    )
    turned_block = pl.pallas_call(
        turn_back,
        name="turn_back",
        out_shape=jax.ShapeDtypeStruct((SIDE * SIDE, C), BF16),
        in_specs=[smem, vmem],
        out_specs=vmem,
    )(rotation, block.reshape(SIDE * SIDE, C))
    return turned_block.reshape(SIDE, SIDE, C)


def solution(mesh):
    in_specs = (P("lat", "lon", None),) + (P(),) * 11
    out_specs = P("lat", "lon", None)
    return jax.shard_map(
        on_device, mesh=mesh, in_specs=in_specs, out_specs=out_specs, check_vma=False
    )
```

```python
import functools
import math

import jax
import jax.numpy as jnp
from jax import lax
from jax.experimental import pallas as pl
from jax.experimental.pallas import tpu as pltpu
from jax.sharding import PartitionSpec as P

MESH = pl.DeviceIdType.MESH
C = 256
HEADS = 4
HEAD_DIM = 64
SIDE = 32
COLS = 512
SEGS = 16
GROUPS = 256
PIECE = 2 * SIDE
BF16 = jnp.bfloat16
F32 = jnp.float32


def row_group(lat, lon):
    pair, core = lat // 2, lat % 2
    z, high = lon // 2, lon % 2
    place = z + high * (15 - 2 * z)
    place = place + (pair % 2) * (15 - 2 * place)
    return 32 * pair + 2 * place + core


def holder(group):
    pair, rest = group // 32, group % 32
    place, core = rest // 2, rest % 2
    place = place + (pair % 2) * (15 - 2 * place)
    high = place // 8
    z = place + high * (15 - 2 * place)
    return 2 * pair + core, 2 * z + high


def turned(block, base, step_i, step_j, first, count):
    cells = lax.broadcasted_iota(jnp.int32, (count, 1), 0) + first
    source = base + step_i * (cells // SIDE) + step_j * (cells % SIDE)
    spots = lax.broadcasted_iota(jnp.int32, (count, SIDE * SIDE), 1)
    pick = jnp.where(spots == source, 1.0, 0.0).astype(BF16)
    return jnp.dot(pick, block, preferred_element_type=F32).astype(BF16)


def steps_of(quarter, upright):
    n = SIDE
    odd_a = (n * (n - 1), 1, -n)
    odd_b = (n - 1, -1, n)
    one, three = (odd_a, odd_b) if upright else (odd_b, odd_a)
    table = [(0, n, 1), one, (n * n - 1, -n, -1), three]

    def chosen(at):
        value = table[0][at]
        for k in (1, 2, 3):
            value = jnp.where(quarter == k, table[k][at], value)
        return value

    return chosen(0), chosen(1), chosen(2)


def section(
    rotation_hbm, owner_hbm, counts_hbm,
    fields_hbm, w1_hbm, b1_hbm, w2_hbm, b2_hbm,
    wq_hbm, wk_hbm, wv_hbm, wo_hbm,
    out_ref,
    rotation_ref, owner_ref, counts_ref, inverse_ref,
    fields_ref, b1_ref, b2_ref, wq_ref, wk_ref, wv_ref, wo_ref,
    upright, raw_up, raw, raw_down, rows, acts, mixed_rows, queries, outgoing, w1, w2, wkv,
    send_in, recv_in, send_halo, recv_halo, send_out, recv_out, local_sem, weight_sem,
    small_sem, partial,
):
    lat, lon = lax.axis_index("lat"), lax.axis_index("lon")
    group = row_group(lat, lon)
    band = group // 16
    mine = band == lat
    barrier = pltpu.get_barrier_semaphore()

    def small_copies():
        pairs = (
            (rotation_hbm, rotation_ref), (fields_hbm, fields_ref),
            (owner_hbm, owner_ref), (counts_hbm, counts_ref),
            (wk_hbm, wk_ref), (wv_hbm, wv_ref),
            (b1_hbm, b1_ref), (b2_hbm, b2_ref), (wq_hbm, wq_ref), (wo_hbm, wo_ref),
        )
        for at, (source, target) in enumerate(pairs):
            yield pltpu.make_async_copy(source, target, small_sem.at[at])

    early = list(small_copies())
    for copy in early[:2]:
        copy.start()

    def greet(device):
        @pl.when(jnp.logical_or(device[0] != lat, device[1] != lon))
        def _():
            pl.semaphore_signal(barrier, inc=1, device_id=device, device_id_type=MESH)

    def greet_all(j, carry):
        greet(holder(16 * lat + j))
        greet((band, j))
        return carry

    lax.fori_loop(0, 16, greet_all, 0)

    @pl.when(group > 0)
    def _():
        pl.semaphore_signal(barrier, inc=1, device_id=holder(group - 1), device_id_type=MESH)

    @pl.when(group < GROUPS - 1)
    def _():
        pl.semaphore_signal(barrier, inc=1, device_id=holder(group + 1), device_id_type=MESH)

    def weight_copies():
        for which, (source, target) in enumerate(((w1_hbm, w1), (w2_hbm, w2))):
            for i in range(3):
                for j in range(3):
                    yield pltpu.make_async_copy(
                        source.at[i, j],
                        target.at[pl.ds(C * i, C), pl.ds(C * j, C)],
                        weight_sem.at[which, 3 * i + j],
                    )

    for copy in early[2:]:
        copy.start()
    for copy in weight_copies():
        copy.start()
    for copy in early[:2]:
        copy.wait()

    quarter = rotation_ref[lat, lon]
    base, step_i, step_j = steps_of(quarter, True)

    def turn(at, carry):
        part = turned(fields_ref[...], base, step_i, step_j, at * 256, 256)
        upright[pl.ds(4 * at, 4)] = part.reshape(4, PIECE, C)
        return carry

    begin = group % 16 // 4
    turn(begin, 0)

    def invert(t, carry):
        for slot in range(3):
            from_band = jnp.clip(group - 1 + slot, 0, GROUPS - 1) // 16
            terms = [
                jnp.where(owner_ref[from_band, s] == t, s, 0) for s in range(1, SEGS)
            ]
            while len(terms) > 1:
                terms = [
                    terms[k] + terms[k + 1] if k + 1 < len(terms) else terms[k]
                    for k in range(0, len(terms), 2)
                ]
            inverse_ref[slot, t] = jnp.minimum(terms[0], SEGS - 1)
        return carry


    own = jnp.where(mine, 1, 0)
    pl.semaphore_wait(
        barrier,
        2 * (16 - own) + jnp.where(group > 0, 1, 0) + jnp.where(group < GROUPS - 1, 1, 0),
    )

    def piece_copy(j):
        return pltpu.make_async_remote_copy(
            src_ref=upright.at[j],
            dst_ref=raw.at[lon],
            send_sem=send_in.at[j],
            recv_sem=recv_in.at[lon],
            device_id=holder(16 * lat + j),
            device_id_type=MESH,
        )

    def own_copy():
        return pltpu.make_async_copy(upright.at[group % 16], raw.at[lon], local_sem.at[0])

    def send_piece(j, carry):

        @pl.when(16 * lat + j != group)
        def _():
            piece_copy(j).start()

        return carry

    lax.fori_loop(4 * begin, 4 * begin + 4, send_piece, 0)

    @pl.when(mine)
    def _():
        own_copy().start()

    def turn_and_send(step, carry):
        at = (begin + step) % 4
        turn(at, 0)
        return lax.fori_loop(4 * at, 4 * at + 4, send_piece, carry)

    lax.fori_loop(1, 4, turn_and_send, 0)

    @pl.when(group == 0)
    def _():
        raw_up[...] = jnp.zeros((SEGS, PIECE, C), BF16)

    @pl.when(group == GROUPS - 1)
    def _():
        raw_down[...] = jnp.zeros((SEGS, PIECE, C), BF16)

    for copy in early[2:6]:
        copy.wait()
    key_part = wk_ref[...]
    value_part = wv_ref[...]
    blank = jnp.zeros((HEAD_DIM, C), BF16)
    wkv[...] = jnp.concatenate(
        [key_part, blank, blank, key_part, value_part, blank, blank, value_part], axis=0
    ).T

    lax.fori_loop(0, SEGS, invert, 0)

    def halo_copy(s, up):
        slot = 2 if up else 0
        return pltpu.make_async_remote_copy(
            src_ref=raw.at[s],
            dst_ref=(raw_down if up else raw_up).at[s],
            send_sem=send_halo.at[slot, s],
            recv_sem=recv_halo.at[slot, s],
            device_id=holder(group - 1 if up else group + 1),
            device_id_type=MESH,
        )

    def arrived(s):
        return pltpu.make_async_remote_copy(
            src_ref=upright.at[0],
            dst_ref=raw.at[s],
            send_sem=send_in.at[0],
            recv_sem=recv_in.at[s],
            device_id=(band, s),
            device_id_type=MESH,
        )

    def forward(t, carry):
        s = (lon + t) % 16
        here = jnp.logical_and(mine, s == lon)

        @pl.when(here)
        def _():
            own_copy().wait()

        @pl.when(jnp.logical_not(here))
        def _():
            arrived(s).wait_recv()

        @pl.when(group > 0)
        def _():
            halo_copy(s, True).start()

        @pl.when(group < GROUPS - 1)
        def _():
            halo_copy(s, False).start()

        return carry

    lax.fori_loop(0, 16, forward, 0)

    def place(slot):
        for t in range(SEGS):
            s = inverse_ref[slot, t]
            piece = (raw_up, raw, raw_down)[slot][s]
            for r in range(2):
                rows[pl.ds(SIDE * t, SIDE), pl.ds(C * (2 * slot + r), C)] = piece[
                    SIDE * r : SIDE * (r + 1)
                ]

    place(1)
    for copy in early[6:]:
        copy.wait()
    for copy in weight_copies():
        copy.wait()

    def mixed_taps(source, r, weight, low_tap, high_tap):
        taps = jnp.dot(
            source[:, C * (r + low_tap) : C * (r + high_tap)],
            weight[C * low_tap : C * high_tap],
            preferred_element_type=F32,
        )
        return (
            pltpu.roll(taps[:, :C], 1, 0)
            + taps[:, C : 2 * C]
            + pltpu.roll(taps[:, 2 * C :], COLS - 1, 0)
        )

    for r, (low_tap, high_tap) in enumerate(((2, 3), (1, 3), (0, 2), (0, 1))):
        partial[r] = mixed_taps(rows, r, w1, low_tap, high_tap) + b1_ref[...]

    def wait_halo(s, carry):
        @pl.when(group < GROUPS - 1)
        def _():
            halo_copy(s, True).wait_recv()

        @pl.when(group > 0)
        def _():
            halo_copy(s, False).wait_recv()

        return carry

    lax.fori_loop(0, 16, wait_halo, 0)
    place(0)
    place(2)

    columns = lax.broadcasted_iota(jnp.int32, (COLS, 1), 0)

    def live_of(offset):
        row = 2 * group + offset
        inside = jnp.logical_and(row >= 0, row < 2 * GROUPS)
        count = jnp.where(inside, counts_ref[jnp.clip(row, 0, 2 * GROUPS - 1)], 0)
        return jnp.where(columns < count, 1.0, 0.0)

    def make_act(r):
        low_tap, high_tap = ((0, 2), (0, 1), (2, 3), (1, 3))[r]
        first = mixed_taps(rows, r, w1, low_tap, high_tap) + partial[r]
        value = first / (1.0 + jnp.exp(-first))
        acts[:, C * r : C * (r + 1)] = (value * live_of(r - 1)).astype(BF16)

    scale = math.log2(math.e) / math.sqrt(HEAD_DIM)
    lanes = lax.broadcasted_iota(jnp.int32, (1, 2 * HEAD_DIM), 1)
    low = lanes < HEAD_DIM
    marks = [
        jnp.where(lanes == (0 if odd else HEAD_DIM), 1.0, 0.0) for odd in range(2)
    ]

    def make_row(r):
        live = live_of(r)
        second = mixed_taps(acts, r, w2, 0, 3) + b2_ref[...]
        grid = rows[:, C * (r + 2) : C * (r + 3)].astype(F32)
        mixed = ((grid + second) * live).astype(BF16)
        flat = mixed.astype(F32)
        mean = jnp.mean(flat * flat, axis=1, keepdims=True)
        normed = (flat * lax.rsqrt(mean + 1e-06)).astype(BF16)
        query = jnp.dot(normed, wq_ref[...], preferred_element_type=F32)
        mixed_rows[r] = mixed.reshape(SEGS, SIDE, C)
        queries[r] = query.astype(BF16).reshape(SEGS, SIDE, C)
        key_val = jnp.dot(normed, wkv[...], preferred_element_type=F32)
        bias = jnp.where(live > 0, 0.0, -1e30)
        ones = jnp.broadcast_to(live, (COLS, 2 * HEAD_DIM)).astype(BF16)
        keys, values = [], []
        for odd in range(2):
            pair = key_val[:, 128 * odd : 128 * (odd + 1)]
            keys.append((pair + bias * marks[odd]).astype(BF16))
            pair = key_val[:, 256 + 128 * odd : 256 + 128 * (odd + 1)].astype(BF16)
            values.append(jnp.concatenate([pair, ones], axis=1))
        count = counts_ref[2 * group + r]
        for offsets in ((3, 5), (4, 0), (2, 6), (1, 7)):
            shards = [
                2 * ((lon // 2 + offset) % 8) + high for offset in offsets for high in range(2)
            ]
            make_chunk(r, shards, count, keys, values)

    cells = lax.broadcasted_iota(jnp.int32, (SIDE, 1), 0)

    def make_chunk(r, shards, count, keys, values):
        segs = [owner_ref[band, s] for s in shards]
        query = jnp.concatenate([queries[r, t] for t in segs], axis=0)
        mixed = jnp.concatenate([mixed_rows[r, t] for t in segs], axis=0)
        live = jnp.concatenate(
            [jnp.where(cells + SIDE * t < count, 1.0, 0.0) for t in segs], axis=0
        )
        size = 4 * SIDE
        halves = []
        for odd in range(2):
            keep = jnp.logical_not(low) if odd else low
            heads = jnp.concatenate([query[:, :128], query[:, 128:]], axis=0)
            heads = jnp.where(keep, heads, marks[odd].astype(BF16))
            scores = lax.dot_general(
                heads, keys[odd], (((1,), (1,)), ((), ())), preferred_element_type=F32
            )
            peak = jnp.max(scores, axis=1, keepdims=True)
            weights = jnp.exp2((scores - peak) * scale).astype(BF16)
            summed = jnp.dot(weights, values[odd], preferred_element_type=F32)
            halves.append(summed[:, :128] / summed[:, 128:])
        both = halves[0] + halves[1]
        attended = jnp.concatenate([both[:size], both[size:]], axis=1).astype(BF16)
        update = jnp.dot(attended, wo_ref[...], preferred_element_type=F32)
        done = (mixed.astype(F32) + update * live).astype(BF16).reshape(4, SIDE, C)
        for k, s in enumerate(shards):
            outgoing[r, s] = done[k]
        for s in shards:
            here = jnp.logical_and(mine, s == lon)

            @pl.when(here)
            def _():
                return_own(r).start()

            @pl.when(jnp.logical_not(here))
            def _():
                return_copy(r, s).start()

    def return_copy(r, s):
        return pltpu.make_async_remote_copy(
            src_ref=outgoing.at[r, s],
            dst_ref=out_ref.at[group % 16, pl.ds(SIDE * r, SIDE)],
            send_sem=send_out.at[r, s],
            recv_sem=recv_out.at[r, group % 16],
            device_id=(band, s),
            device_id_type=MESH,
        )

    def return_own(r):
        return pltpu.make_async_copy(
            outgoing.at[r, lon],
            out_ref.at[group % 16, pl.ds(SIDE * r, SIDE)],
            local_sem.at[1 + r],
        )

    for r in range(3):
        make_act(r)
    make_row(0)
    make_act(3)
    make_row(1)

    def drain(t, carry):
        @pl.when(16 * lat + t != group)
        def _():
            piece_copy(t).wait_send()

        @pl.when(group > 0)
        def _():
            halo_copy(t, True).wait_send()

        @pl.when(group < GROUPS - 1)
        def _():
            halo_copy(t, False).wait_send()

        @pl.when(jnp.logical_or(band != lat, t != lon))
        def _():
            for r in range(2):
                return_copy(r, t).wait_send()

        @pl.when(16 * lat + t != group)
        def _():
            for r in range(2):
                pltpu.make_async_remote_copy(
                    src_ref=outgoing.at[r, 0],
                    dst_ref=out_ref.at[t, pl.ds(SIDE * r, SIDE)],
                    send_sem=send_out.at[r, 0],
                    recv_sem=recv_out.at[r, t],
                    device_id=holder(16 * lat + t),
                    device_id_type=MESH,
                ).wait_recv()

        return carry

    lax.fori_loop(0, 16, drain, 0)

    @pl.when(mine)
    def _():
        for r in range(2):
            return_own(r).wait()


def turn_back(rotation_ref, block_ref, out_ref):
    quarter = rotation_ref[lax.axis_index("lat"), lax.axis_index("lon")]
    base, step_i, step_j = steps_of(quarter, False)

    out_ref[...] = turned(
        block_ref[...], base, step_i, step_j, pl.program_id(0) * 256, 256
    )


def on_device(
    fields, w_conv1, b_conv1, w_conv2, b_conv2, w_query, w_key, w_value, w_out,
    rotation, owner, counts,
):
    smem = pl.BlockSpec(memory_space=pltpu.SMEM)
    vmem = pl.BlockSpec(memory_space=pltpu.VMEM)
    hbm = pl.BlockSpec(memory_space=pltpu.HBM)
    dma = pltpu.SemaphoreType.DMA
    block = pl.pallas_call(
        section,
        name="section",
        out_shape=jax.ShapeDtypeStruct((SEGS, PIECE, C), BF16),
        in_specs=[hbm] * 12,
        out_specs=vmem,
        scratch_shapes=[
            pltpu.SMEM((16, 16), jnp.int32),
            pltpu.SMEM((16, 16), jnp.int32),
            pltpu.SMEM((2 * GROUPS,), jnp.int32),
            pltpu.SMEM((3, SEGS), jnp.int32),
            pltpu.VMEM((SIDE * SIDE, C), BF16),
            pltpu.VMEM((1, C), F32),
            pltpu.VMEM((1, C), F32),
            pltpu.VMEM((C, C), BF16),
            pltpu.VMEM((HEAD_DIM, C), BF16),
            pltpu.VMEM((HEAD_DIM, C), BF16),
            pltpu.VMEM((C, C), BF16),
            pltpu.VMEM((SEGS, PIECE, C), BF16),
            pltpu.VMEM((SEGS, PIECE, C), BF16),
            pltpu.VMEM((SEGS, PIECE, C), BF16),
            pltpu.VMEM((SEGS, PIECE, C), BF16),
            pltpu.VMEM((COLS, 6 * C), BF16),
            pltpu.VMEM((COLS, 4 * C), BF16),
            pltpu.VMEM((2, SEGS, SIDE, C), BF16),
            pltpu.VMEM((2, SEGS, SIDE, C), BF16),
            pltpu.VMEM((2, SEGS, SIDE, C), BF16),
            pltpu.VMEM((3 * C, 3 * C), BF16),
            pltpu.VMEM((3 * C, 3 * C), BF16),
            pltpu.VMEM((C, 8 * HEAD_DIM), BF16),
            dma((16,)),
            dma((16,)),
            dma((3, 16)),
            dma((3, 16)),
            dma((2, 16)),
            dma((2, 16)),
            dma((3,)),
            dma((2, 9)),
            dma((10,)),
            pltpu.VMEM((4, COLS, C), F32),
        ],
        compiler_params=pltpu.CompilerParams(
            collective_id=0, has_side_effects=True, vmem_limit_bytes=67043328
        ),
    )(
        rotation, owner, counts,
        fields.reshape(SIDE * SIDE, C), w_conv1, b_conv1.reshape(1, C), w_conv2,
        b_conv2.reshape(1, C), w_query, w_key.T, w_value.T, w_out,
    )
    turned_block = pl.pallas_call(
        turn_back,
        name="turn_back",
        out_shape=jax.ShapeDtypeStruct((SIDE * SIDE, C), BF16),
        grid=(4,),
        in_specs=[smem, pl.BlockSpec((SIDE * SIDE, C), lambda at: (0, 0))],
        out_specs=pl.BlockSpec((256, C), lambda at: (at, 0)),
    )(rotation, block.reshape(SIDE * SIDE, C))
    return turned_block.reshape(SIDE, SIDE, C)


def solution(mesh):
    in_specs = (P("lat", "lon", None),) + (P(),) * 11
    out_specs = P("lat", "lon", None)
    return jax.shard_map(
        on_device, mesh=mesh, in_specs=in_specs, out_specs=out_specs, check_vma=False
    )
```
